32 devices in a mesh: site: 2 (over y), gx: 4 (over z), gy: 2 (over x), comp: 2 (over core).
Axes of the slice: x: 2, y: 2, z: 4, core: 2. Of those that a mesh axis runs over, the one named last changes fastest.
Arguments:
- displacement: float32 [2, 3, 32, 64, 128], P('comp', None, ('site', 'gx'), 'gy'), parts along dimension 2, may hold values from -6 to 6
- previous: float32 [2, 3, 32, 64, 128], P('comp', None, ('site', 'gx'), 'gy'), parts along dimension 2, may hold values from -6 to 6
- first_lame: float32 [32, 64, 128], P(('site', 'gx'), 'gy'), parts along dimension 0, may hold values from 0.5 to 2
- shear_modulus: float32 [32, 64, 128], P(('site', 'gx'), 'gy'), parts along dimension 0, may hold values from 0.5 to 2
- buoyancy: float32 [32, 64, 128], P(('site', 'gx'), 'gy'), parts along dimension 0, may hold values from 0.5 to 2
- tile_column: int32 [2048], P(('site', 'gx', 'gy')), parts along dimension 0, may hold values from 0 to 127
- rupture_tiles: int32 [256, 16], P(('site', 'gx', 'gy')), parts along dimension 0, may hold values from 0 to 1023, as said below
- slip_offsets: int32 [256, 16], P(('site', 'gx', 'gy')), parts along dimension 0, may hold values from 0 to 3
- slip_panels: bfloat16 [256, 16, 6, 128], P(('site', 'gx', 'gy')), parts along dimension 0, may hold values from -0.0546875 to 0.0546875
Outputs:
- final_displacement: float32 [2, 3, 32, 64, 128], P('comp', None, ('site', 'gx'), 'gy'), parts along dimension 2
- synthetics: float32 [2, 256, 4], P('comp', ('site', 'gx', 'gy')), parts along dimension 1
The draws below stay inside these ranges and needn't reach their ends.
There are 2 independent parts, one for each index of `site`. The reference program is written for one: setup_inputs(seed, part) draws one part's arguments, and reference() takes and returns one part's arrays. A program takes and returns all parts, laid end to end along the dimension named above; each array names one. Nothing has to cross between parts.
Inputs may be any that keep to these rules, and one draw needn't show every extreme that they name: `rupture_tiles`: of the 16 x 16 entries of the ruptures r with the same r // 16, between 1 and 64 name tiles t with the same t // 128, for every such device; in each such group some device is named exactly 64 times. Entries may repeat; each group names tile 0 and tile 1024 - 1.
All inputs are finite; a program needn't handle non-finite values.
Results may differ from the reference program's by a relative error of at most 0.0027.
Values may be sent and summed in bfloat16 or wider, within the bound.
No kernel may reach another device: no remote copies, remote signals or barrier semaphores. Data moves between devices by JAX's collectives and lax.ppermute only.
A program may use at most 64 MiB of HBM per device.

```python
import math
import jax
import jax.numpy as jnp
from jax import lax

CX = 4
CY = 32
NZ = 128
STEPS = 4
TILE_DEV = 128
RUP_DEV = 16
LIST = 16
NX = 16
NY = 64
OWNERS = 8
CAP = 64
TILES = 1024
RUPTURES = 128
N_GY = 2


def owner_entries(key):
    total = RUP_DEV * LIST
    extra = total - OWNERS
    room = CAP - 1
    keys = jax.random.split(key, 4)
    slot_ids = jnp.arange(OWNERS * room, dtype=jnp.int32)
    owner_of = slot_ids // room
    heavy = jax.random.randint(keys[1], (), 0, OWNERS, dtype=jnp.int32)
    scores = jax.random.permutation(keys[0], OWNERS * room).astype(jnp.int32)
    scores = jnp.where(owner_of == heavy, slot_ids % room - room, scores)
    order = jnp.argsort(scores, stable=True)
    chosen = owner_of[order[:extra]]
    counts = 1 + jnp.sum((chosen[:, None] == jnp.arange(OWNERS, dtype=jnp.int32)[None, :]).astype(jnp.int32), axis=0)
    sources = jnp.repeat(jnp.arange(OWNERS, dtype=jnp.int32), counts, total_repeat_length=total)
    sources = jax.random.permutation(keys[2], sources)
    slots = jax.random.randint(keys[3], (total,), 0, TILE_DEV, dtype=jnp.int32)
    positions = jnp.arange(total, dtype=jnp.int32)
    slots = jnp.where(positions == jnp.argmax(sources), TILE_DEV - 1, slots)
    slots = jnp.where(positions == jnp.argmin(sources), 0, slots)
    return (sources * TILE_DEV + slots).astype(jnp.int32).reshape(RUP_DEV, LIST)


def draw_rupture_tiles(key, part):
    keys = jax.random.split(jax.random.fold_in(key, 17), OWNERS)
    return jax.vmap(owner_entries)(keys).reshape(RUP_DEV * OWNERS, LIST)


def place_ends(entries, rng, least, high):
    index_at = [jax.random.randint(jax.random.fold_in(rng, axis), (), 0, length) for axis, length in enumerate(entries.shape)]
    main_axis = entries.shape.index(max(entries.shape))
    neighbour = index_at[:main_axis] + [(index_at[main_axis] + 1) % entries.shape[main_axis]] + index_at[main_axis + 1:]
    return entries.at[tuple(index_at)].set(least).at[tuple(neighbour)].set(high)


def level_of(rng, extent, pieces, least, largest):
    loudness = 1.0
    for dim, blocks in pieces:
        steps = jax.random.uniform(jax.random.fold_in(jax.random.fold_in(rng, 6), dim), (blocks,), jnp.float32, least / len(pieces), largest / len(pieces))
        loudness = loudness * jnp.repeat(jnp.exp(steps), extent[dim] // blocks).reshape((-1,) + (1,) * (len(extent) - 1 - dim))
    return loudness


def gaussian(stream_key, shape, spread, limit, pieces=(), held_as=jnp.bfloat16):
    result = jax.random.normal(stream_key, shape, jnp.float32) * spread
    if len(pieces) > 0:
        result = level_of(stream_key, shape, pieces, -0.22, 0.18) * result
    return jnp.clip(result, min=-limit, max=limit).astype(held_as)


def setup_inputs(seed: int = 0, part: int = 0) -> dict:
    key_of = jax.random.split(jax.random.key(seed), 10)
    own_keys = jax.random.split(jax.random.fold_in(key_of[9], part), 10)
    displacement = gaussian(own_keys[0], (2, 3, NX, NY, NZ), 1.0, 6.0, ((0, 2), (2, 4), (3, 2)), jnp.float32)
    previous = gaussian(own_keys[1], (2, 3, NX, NY, NZ), 1.0, 6.0, ((0, 2), (2, 4), (3, 2)), jnp.float32)
    first_lame = jnp.clip(jnp.exp(math.log(2.0) - 1.3862944 * jax.random.uniform(own_keys[2], (NX, NY, NZ), jnp.float32) ** level_of(own_keys[2], (NX, NY, NZ), ((0, 4), (1, 2)), -0.2, 0.2)), 0.5, 2.0)
    shear_modulus = jnp.clip(jnp.exp(math.log(2.0) - 1.3862944 * jax.random.uniform(own_keys[3], (NX, NY, NZ), jnp.float32) ** level_of(own_keys[3], (NX, NY, NZ), ((0, 4), (1, 2)), -0.2, 0.2)), 0.5, 2.0)
    buoyancy = jnp.clip(jnp.exp(math.log(2.0) - 1.3862944 * jax.random.uniform(own_keys[4], (NX, NY, NZ), jnp.float32) ** level_of(own_keys[4], (NX, NY, NZ), ((0, 4), (1, 2)), -0.2, 0.2)), 0.5, 2.0)
    tile_column = place_ends(jax.random.randint(own_keys[5], (TILES,), 0, CX * CY), jax.random.fold_in(own_keys[5], 1), 0, (CX * CY) - 1).astype(jnp.int32)
    rupture_tiles = draw_rupture_tiles(jax.random.fold_in(jax.random.fold_in(key_of[9], part), 71), part)
    slip_offsets = place_ends(jax.random.randint(own_keys[7], (RUPTURES, LIST), 0, STEPS), jax.random.fold_in(own_keys[7], 1), 0, STEPS - 1).astype(jnp.int32)
    slip_panels = gaussian(own_keys[8], (RUPTURES, LIST, 6, NZ), (LIST * 6 * NZ) ** -0.5, 0.0546875, ((0, 8),))
    return dict(displacement=displacement, previous=previous, first_lame=first_lame, shear_modulus=shear_modulus, buoyancy=buoyancy, tile_column=tile_column, rupture_tiles=rupture_tiles, slip_offsets=slip_offsets, slip_panels=slip_panels)


time_step = 0.12


def forward_difference(values, direction):
    widths = [(0, 0), (0, 0), (0, 0)]
    widths[direction] = (0, 1)
    padded = jnp.pad(values, widths)
    return lax.slice_in_dim(padded, 1, values.shape[direction] + 1, axis=direction) - values


def backward_difference(values, direction):
    widths = [(0, 0), (0, 0), (0, 0)]
    widths[direction] = (1, 0)
    padded = jnp.pad(values, widths)
    return values - lax.slice_in_dim(padded, 0, values.shape[direction], axis=direction)


def strain_field(current):
    gradients = [[forward_difference(current[comp_index], direction) for direction in range(3)] for comp_index in range(3)]
    return [gradients[0][0], gradients[1][1], gradients[2][2],
            0.5 * (gradients[0][1] + gradients[1][0]),
            0.5 * (gradients[0][2] + gradients[2][0]),
            0.5 * (gradients[1][2] + gradients[2][1])]


def stress_field(strains, first_lame, shear_modulus):
    trace = strains[0] + strains[1] + strains[2]
    twice = 2.0 * shear_modulus
    return [first_lame * trace + twice * strains[0],
            first_lame * trace + twice * strains[1],
            first_lame * trace + twice * strains[2],
            twice * strains[3], twice * strains[4], twice * strains[5]]


def advance(current, earlier, first_lame, shear_modulus, buoyancy):
    strains = strain_field(current)
    stresses = stress_field(strains, first_lame, shear_modulus)
    forces = [backward_difference(stresses[0], 0) + backward_difference(stresses[3], 1) + backward_difference(stresses[4], 2),
              backward_difference(stresses[3], 0) + backward_difference(stresses[1], 1) + backward_difference(stresses[5], 2),
              backward_difference(stresses[4], 0) + backward_difference(stresses[5], 1) + backward_difference(stresses[2], 2)]
    step_scale = time_step * time_step * buoyancy
    updated = jnp.stack([2.0 * current[comp_index] - earlier[comp_index] + step_scale * forces[comp_index] for comp_index in range(3)])
    return updated, strains


def reference(displacement, previous, first_lame, shear_modulus, buoyancy, tile_column, rupture_tiles, slip_offsets, slip_panels):
    tile_ids = jnp.arange(TILES, dtype=jnp.int32)
    device_index = tile_ids // TILE_DEV
    first_index = (device_index // N_GY) * CX + tile_column // CY
    second_index = (device_index % N_GY) * CY + tile_column % CY
    slip_flat = slip_panels.reshape(RUPTURES * LIST, 6 * NZ).astype(jnp.float32)
    flat_tiles = rupture_tiles.reshape(RUPTURES * LIST)
    lag_table = jnp.arange(STEPS, dtype=jnp.int32)[None, None, :] - jnp.arange(STEPS, dtype=jnp.int32)[None, :, None]
    select = (slip_offsets.reshape(RUPTURES * LIST)[:, None, None] == lag_table).astype(jnp.float32)
    finals = []
    synthetic_list = []
    for component in range(2):
        current = displacement[component]
        earlier = previous[component]
        responses = []
        for instant in range(STEPS):
            updated, strains = advance(current, earlier, first_lame, shear_modulus, buoyancy)
            tile_strain = jnp.stack([strain[first_index, second_index, :] for strain in strains], axis=1)
            tile_strain = tile_strain.astype(jnp.bfloat16).reshape(TILES, 6 * NZ)
            picked = tile_strain[flat_tiles].astype(jnp.float32)
            responses.append(jnp.sum(picked * slip_flat, axis=1))
            earlier, current = current, updated
        response = jnp.stack(responses, axis=1)
        delayed = jnp.sum(response[:, :, None] * select, axis=1)
        synthetic_list.append(delayed.reshape(RUPTURES, LIST, STEPS).sum(axis=1))
        finals.append(current)
    return jnp.stack(finals), jnp.stack(synthetic_list)
```

```python
import functools

import jax
import jax.numpy as jnp
from jax import lax
from jax.experimental import pallas as pl
from jax.experimental.pallas import tpu as pltpu
from jax.sharding import PartitionSpec as P

STEPS = 4
TIME_STEP = 0.12
LANES = 128
PAD = 8
OWNERS_AXES = ("gx", "gy")
NT = (((1,), (1,)), ((), ()))


def iota(shape, dim):
    return lax.broadcasted_iota(jnp.int32, shape, dim)


def owner_index():
    return lax.axis_index("gx") * lax.axis_size("gy") + lax.axis_index("gy")


def pack_kernel(owners, slots, ranks, tiles_ref, offsets_ref, panels_ref, out_ref, meta_ref):
    rows, cols = tiles_ref.shape
    entries = rows * cols
    core = lax.axis_index("comp")
    me = owner_index()
    tiles = tiles_ref[...]
    shift = slots.bit_length() - 1
    fields = jnp.concatenate([tiles >> shift, tiles & (slots - 1), offsets_ref[...]], axis=0)
    spread = (iota((cols, entries), 1) % cols == iota((cols, entries), 0)).astype(jnp.bfloat16)
    wide = jnp.dot(fields.astype(jnp.float32).astype(jnp.bfloat16), spread, preferred_element_type=jnp.float32)
    lane_row = iota((rows, entries), 1) // cols
    keep = lane_row == iota((rows, entries), 0)
    source, slot, offset = [
        jnp.sum(jnp.where(keep, wide[i * rows : (i + 1) * rows], 0.0), axis=0, keepdims=True) for i in range(3)
    ]
    record = (iota((1, entries), 1) // cols).astype(jnp.float32) * STEPS + offset
    chosen = source == iota((owners, entries), 0).astype(jnp.float32)
    before = (iota((entries, entries), 0) < iota((entries, entries), 1)).astype(jnp.bfloat16)
    counts = jnp.dot(chosen.astype(jnp.bfloat16), before, preferred_element_type=jnp.float32)
    rank = jnp.sum(jnp.where(chosen, counts, 0.0), axis=0, keepdims=True).astype(jnp.int32) - core * ranks
    mine = (rank >= 0) & (rank < ranks)
    place = jnp.where(mine, source.astype(jnp.int32) * ranks + rank, -1)
    sent = owners * ranks
    select = (iota((sent, entries), 0) == place).astype(jnp.bfloat16)
    blocks = out_ref.shape[0]
    length = sent // blocks
    for i in range(panels_ref.shape[0]):
        part = jnp.dot(select, panels_ref[i], preferred_element_type=jnp.float32).astype(jnp.bfloat16)
        out_ref[:, i * length : (i + 1) * length, :] = part.reshape(blocks, length, LANES)
    group = LANES // ranks
    lane = jnp.where(mine, rank + ranks * (me % group), -1)
    marks = (iota((LANES, entries), 0) == lane).astype(jnp.bfloat16)
    for k, value in enumerate((slot, record)):
        table = jnp.where(chosen, value, 0.0).astype(jnp.bfloat16)
        rows_out = lax.dot_general(table, marks, NT, preferred_element_type=jnp.float32).astype(jnp.bfloat16)
        meta_ref[k] = rows_out


def pack(owners, slots, ranks, tiles, offsets, panels):
    friendly = ranks % 16 == 0
    blocks = owners if friendly else 1
    sent = owners * ranks
    components = panels.shape[0]
    body, meta = pl.pallas_call(
        functools.partial(pack_kernel, owners, slots, ranks),
        out_shape=(
            jax.ShapeDtypeStruct((blocks, components * sent // blocks, LANES), jnp.bfloat16),
            jax.ShapeDtypeStruct((2, owners, LANES), jnp.bfloat16),
        ),
        in_specs=[pl.BlockSpec(memory_space=pltpu.VMEM)] * 3,
        out_specs=(pl.BlockSpec(memory_space=pltpu.VMEM),) * 2,
        name="pack",
    )(tiles, offsets, panels)
    if not friendly:
        body = body.reshape(components, owners, ranks, LANES).transpose(1, 0, 2, 3)
        body = body.reshape(owners, components * ranks, LANES)
    return jnp.concatenate([body, meta.transpose(1, 0, 2)], axis=1)


def unpack(owners, ranks, components, arrived):
    body = arrived[:, : components * ranks]
    meta = arrived[:, components * ranks :].transpose(1, 0, 2)
    if ranks % 16:
        body = body.reshape(owners, components, ranks, LANES).transpose(1, 0, 2, 3)
        body = body.reshape(1, components * owners * ranks, LANES)
    return body, meta


def shifted_up(value, dim):
    return pltpu.roll(value, value.shape[dim] - 1, dim)


def stencil_kernel(halo, merged, *refs):
    disp, prev, lam, mu, buoy, x_low, x_high = refs[:7]
    sides = refs[7:13] if not merged else refs[7:10] * 2
    out_ref, strain_ref = refs[-7:-5]
    wave, first, second, scale = refs[-5:-1]
    nx, ny, nz = lam.shape
    tall = ny + 2 * PAD
    gy = lax.axis_index("gy")
    own_x, own_y = pl.ds(halo, nx), pl.ds(PAD, ny)
    lows, highs = pl.ds(0, halo), pl.ds(halo + nx, halo)

    targets = [wave.at[0, i] for i in range(3)] + [wave.at[1, i] for i in range(3)] + [first, second, scale]
    owns = [disp[0, i] for i in range(3)] + [prev[0, i] for i in range(3)] + [lam[...], mu[...], buoy[...]]
    dt2 = TIME_STEP * TIME_STEP
    for f, (target, own) in enumerate(zip(targets, owns)):
        factor = dt2 if f == 8 else None

        def put(xs, ys, value, factor=factor, target=target):
            target[xs, ys, :] = value if factor is None else value * factor

        put(own_x, own_y, own)
        put(lows, own_y, x_low[f])
        put(highs, own_y, x_high[f])
        for s, ys in ((0, pl.ds(PAD - halo, halo)), (1, pl.ds(PAD + ny, halo))):
            middle, low, high = [r[f] for r in sides[3 * s : 3 * s + 3]]
            if merged:
                here = gy == (1 - s)
                middle, low, high = [jnp.where(here, v, 0.0) for v in (middle, low, high)]
            put(own_x, ys, middle)
            put(lows, ys, low)
            put(highs, ys, high)

    lane = iota((tall, nz), 1)
    not_last, not_first = lane < nz - 1, lane > 0

    def fields(cur, x):
        base = [wave[cur, i, x] for i in range(3)]
        nxt = [wave[cur, i, x + 1] for i in range(3)]
        dx = [n - b for n, b in zip(nxt, base)]
        dy = [shifted_up(b, 0) - b for b in base]
        dz = [jnp.where(not_last, shifted_up(b, 1), 0.0) - b for b in base]
        normal = [dx[0], dy[1], dz[2]]
        twice = [dy[0] + dx[1], dz[0] + dx[2], dz[1] + dy[2]]
        m = second[x]
        volume = first[x] * (normal[0] + normal[1] + normal[2])
        m2 = m + m
        stress = [volume + m2 * e for e in normal] + [m * e for e in twice]
        return base, normal, twice, stress

    def back_y(v):
        return v - pltpu.roll(v, 1, 0)

    def back_z(v):
        return v - jnp.where(not_first, pltpu.roll(v, 1, 1), 0.0)

    def plane(step, cur, own, x, carry):
        base, normal, twice, stress = fields(cur, x)
        if own:
            rows = pl.ds(pl.multiple_of(step * nx * ny + (x - halo) * ny, ny), ny)
            for e, value in enumerate(normal + [0.5 * t for t in twice]):
                strain_ref[rows, e * nz : (e + 1) * nz] = value[PAD : PAD + ny].astype(jnp.bfloat16)
        xx, yy, zz, xy, xz, yz = stress
        forces = [
            (xx - carry[0]) + back_y(xy) + back_z(xz),
            (xy - carry[1]) + back_y(yy) + back_z(yz),
            (xz - carry[2]) + back_y(yz) + back_z(zz),
        ]
        for i in range(3):
            value = 2.0 * base[i] - wave[1 - cur, i, x] + scale[x] * forces[i]
            if step == STEPS - 1:
                out_ref[0, i, x - halo] = value[PAD : PAD + ny]
            else:
                wave[1 - cur, i, x] = value
        return xx, xy, xz

    for step in range(STEPS):
        cur = step % 2
        reach = STEPS - 1 - step
        begin, end = halo - reach, halo + nx + reach
        stress = fields(cur, begin - 1)[3]
        carry = (stress[0], stress[3], stress[4])
        for lo, hi, own in ((begin, halo, False), (halo, halo + nx, True), (halo + nx, end, False)):
            if hi > lo:
                carry = lax.fori_loop(lo, hi, functools.partial(plane, step, cur, own), carry)


def stencil(halo, merged, disp, prev, lam, mu, buoy, x_low, x_high, sides):
    nx, ny, nz = lam.shape
    tall, wide = ny + 2 * PAD, nx + 2 * halo
    vmem = pl.BlockSpec(memory_space=pltpu.VMEM)
    operands = (disp, prev, lam, mu, buoy, x_low, x_high, *sides)
    return pl.pallas_call(
        functools.partial(stencil_kernel, halo, merged),
        out_shape=(
            jax.ShapeDtypeStruct(disp.shape, jnp.float32),
            jax.ShapeDtypeStruct((STEPS * nx * ny, 6 * nz), jnp.bfloat16),
        ),
        in_specs=[vmem] * len(operands),
        out_specs=(vmem, vmem),
        scratch_shapes=[pltpu.VMEM((2, 3, wide, tall, nz), jnp.float32)]
        + [pltpu.VMEM((wide, tall, nz), jnp.float32)] * 3
        + [pltpu.SMEM((1,), jnp.int32)],
        compiler_params=pltpu.CompilerParams(vmem_limit_bytes=40 << 20),
        name="stencil",
    )(*operands)


def response_kernel(owners, ranks, records, strain_ref, column_ref, pan0, meta0, pan1, meta1, out_ref):
    points = column_ref.shape[1]
    sent = owners * ranks
    group = LANES // ranks
    columns = strain_ref.shape[0] // STEPS
    total = None
    for pan, meta in ((pan0, meta0), (pan1, meta1)):
        rows = []
        for k in range(2):
            table = meta[k].astype(jnp.float32)
            parts = [
                jnp.sum(table[g * group : (g + 1) * group], axis=0, keepdims=True) for g in range(owners // group)
            ]
            rows.append(jnp.concatenate(parts, axis=1))
        slot, record = rows
        owner = iota((1, sent), 1) // ranks
        spread = (iota((points, sent), 0) == slot.astype(jnp.int32)).astype(jnp.bfloat16)
        table = jnp.broadcast_to(column_ref[...].astype(jnp.float32), (8, points)).astype(jnp.bfloat16)
        column = jnp.dot(table, spread, preferred_element_type=jnp.float32)[:1].astype(jnp.int32)
        length = pan.shape[1] // 6
        grid = None
        for i in range(3):
            right = jnp.concatenate(
                [pan[:, (2 * i + k) * length : (2 * i + k + 1) * length, :].reshape(sent, LANES) for k in range(2)],
                axis=1,
            )
            left = strain_ref[:, 2 * i * LANES : (2 * i + 2) * LANES]
            term = lax.dot_general(left, right, NT, preferred_element_type=jnp.float32)
            grid = term if grid is None else grid + term
        mark = iota((columns, sent), 0) == column
        reply = [
            jnp.sum(jnp.where(mark, grid[m * columns : (m + 1) * columns], 0.0), axis=0, keepdims=True)
            for m in range(STEPS)
        ]
        record = record.astype(jnp.int32)
        offset = record % STEPS
        delayed = []
        for n in range(STEPS):
            value = jnp.where(offset == n, reply[0], 0.0)
            for m in range(1, n + 1):
                value = value + jnp.where(offset == n - m, reply[m], 0.0)
            delayed.append(value)
        delayed = jnp.concatenate(delayed + [jnp.zeros((8 - STEPS, sent), jnp.float32)], axis=0)
        key = owner * records + record // STEPS
        gather = (iota((owners * records, sent), 0) == key).astype(jnp.float32)
        part = lax.dot_general(
            delayed, gather, NT, preferred_element_type=jnp.float32, precision=lax.Precision.HIGHEST
        )
        total = part if total is None else total + part
    out_ref[...] = total[:STEPS]


def respond(owners, ranks, records, strain, columns, halves):
    vmem = pl.BlockSpec(memory_space=pltpu.VMEM)
    operands = (strain, columns, *halves[0], *halves[1])
    return pl.pallas_call(
        functools.partial(response_kernel, owners, ranks, records),
        out_shape=jax.ShapeDtypeStruct((STEPS, owners * records), jnp.float32),
        in_specs=[vmem] * len(operands),
        out_specs=vmem,
        compiler_params=pltpu.CompilerParams(vmem_limit_bytes=40 << 20),
        name="respond",
    )(*operands)


def shift_pairs(nx, ny, dx, dy):
    return [
        (i * ny + j, (i + dx) * ny + j + dy)
        for i in range(nx)
        for j in range(ny)
        if 0 <= i + dx < nx and 0 <= j + dy < ny
    ]


def owner_sum(value, owners):
    if owners & (owners - 1):
        return lax.psum(value, OWNERS_AXES)
    bit = 1
    while bit < owners:
        value = value + lax.ppermute(value, OWNERS_AXES, [(i, i ^ bit) for i in range(owners)])
        bit *= 2
    return value


def body(displacement, previous, first_lame, shear_modulus, buoyancy, tile_column, rupture_tiles, slip_offsets, slip_panels):
    gxs, gys = lax.axis_size("gx"), lax.axis_size("gy")
    owners = gxs * gys
    nx, ny, nz = shear_modulus.shape
    halo = STEPS
    slots = tile_column.shape[0]
    records, listed = rupture_tiles.shape
    entries = records * listed
    ranks = entries // owners
    components = slip_panels.shape[2]

    fields = jnp.concatenate(
        [displacement[0], previous[0], first_lame[None], shear_modulus[None], buoyancy[None]], axis=0
    )
    merged = gys == 2
    gy = lax.axis_index("gy")

    def send(value, dx, dy):
        pairs = shift_pairs(gxs, gys, dx, dy)
        if merged and dy:
            pairs = pairs + shift_pairs(gxs, gys, dx, -dy)
        return lax.ppermute(value, OWNERS_AXES, pairs)

    x_low = send(fields[:, nx - halo :], 1, 0)
    x_high = send(fields[:, :halo], -1, 0)
    if merged:
        edge = lax.dynamic_slice_in_dim(fields, jnp.where(gy == 0, ny - halo, 0), halo, axis=2)
        sides = [send(edge, 0, 1), send(edge, 1, 1), send(edge, -1, 1)]
    else:
        upper, lower = fields[:, :, ny - halo :], fields[:, :, :halo]
        sides = [send(upper, dx, 1) for dx in (0, 1, -1)] + [send(lower, dx, -1) for dx in (0, 1, -1)]

    panels = slip_panels.reshape(entries, components, nz).transpose(1, 0, 2)
    payload = pack(owners, slots, ranks, rupture_tiles, slip_offsets, panels)
    arrived = lax.all_to_all(payload, OWNERS_AXES, split_axis=0, concat_axis=0, tiled=True)
    other = lax.ppermute(arrived, "comp", [(0, 1), (1, 0)])

    final, strain = stencil(
        halo, merged, displacement, previous, first_lame, shear_modulus, buoyancy, x_low, x_high, sides
    )
    halves = [unpack(owners, ranks, components, v) for v in (arrived, other)]
    partial = respond(owners, ranks, records, strain, tile_column.reshape(1, slots), halves)
    summed = owner_sum(partial, owners)
    mine = lax.dynamic_slice_in_dim(summed, owner_index() * records, records, axis=1)
    return final, mine.T[None]


def solution(mesh):
    in_specs = (
        P("comp", None, ("site", "gx"), "gy", None),
        P("comp", None, ("site", "gx"), "gy", None),
        P(("site", "gx"), "gy", None),
        P(("site", "gx"), "gy", None),
        P(("site", "gx"), "gy", None),
        P(("site", "gx", "gy")),
        P(("site", "gx", "gy"), None),
        P(("site", "gx", "gy"), None),
        P(("site", "gx", "gy"), None, None, None),
    )
    out_specs = (P("comp", None, ("site", "gx"), "gy", None), P("comp", ("site", "gx", "gy"), None))
    return jax.shard_map(body, mesh=mesh, in_specs=in_specs, out_specs=out_specs, check_vma=False)
```

```python
import functools

import jax
import jax.numpy as jnp
from jax import lax
from jax.experimental import pallas as pl
from jax.experimental.pallas import tpu as pltpu
from jax.sharding import PartitionSpec as P

STEPS = 4
TIME_STEP = 0.12
LANES = 128
PAD = 8
OWNERS_AXES = ("gx", "gy")
FIELDS = 9
NT = (((1,), (1,)), ((), ()))


def iota(shape, dim):
    return lax.broadcasted_iota(jnp.int32, shape, dim)


def owner_index():
    return lax.axis_index("gx") * lax.axis_size("gy") + lax.axis_index("gy")


def pack_kernel(owners, slots, ranks, tiles_ref, offsets_ref, panels_ref, out_ref, meta_ref=None):
    rows, cols = tiles_ref.shape
    entries = rows * cols
    core = lax.axis_index("comp")
    me = owner_index()
    tiles = tiles_ref[...]
    shift = slots.bit_length() - 1
    fields = jnp.concatenate([tiles >> shift, tiles & (slots - 1), offsets_ref[...]], axis=0)
    spread = (iota((cols, entries), 1) % cols == iota((cols, entries), 0)).astype(jnp.bfloat16)
    wide = jnp.dot(fields.astype(jnp.float32).astype(jnp.bfloat16), spread, preferred_element_type=jnp.float32)
    lane_row = iota((rows, entries), 1) // cols
    keep = lane_row == iota((rows, entries), 0)
    source, slot, offset = [
        jnp.sum(jnp.where(keep, wide[i * rows : (i + 1) * rows], 0.0), axis=0, keepdims=True) for i in range(3)
    ]
    record = (iota((1, entries), 1) // cols).astype(jnp.float32) * STEPS + offset
    chosen = source == iota((owners, entries), 0).astype(jnp.float32)
    before = (iota((entries, entries), 0) < iota((entries, entries), 1)).astype(jnp.bfloat16)
    counts = jnp.dot(chosen.astype(jnp.bfloat16), before, preferred_element_type=jnp.float32)
    rank = jnp.sum(jnp.where(chosen, counts, 0.0), axis=0, keepdims=True).astype(jnp.int32) - core * ranks
    mine = (rank >= 0) & (rank < ranks)
    place = jnp.where(mine, source.astype(jnp.int32) * ranks + rank, -1)
    sent = owners * ranks
    select = (iota((sent, entries), 0) == place).astype(jnp.bfloat16)
    blocks = out_ref.shape[0]
    length = sent // blocks
    for i in range(panels_ref.shape[0]):
        part = jnp.dot(select, panels_ref[i], preferred_element_type=jnp.float32).astype(jnp.bfloat16)
        out_ref[:, i * length : (i + 1) * length, :] = part.reshape(blocks, length, LANES)
    group = LANES // ranks
    lane = jnp.where(mine, rank + ranks * (me % group), -1)
    marks = (iota((LANES, entries), 0) == lane).astype(jnp.bfloat16)
    meta = []
    for value in (slot, record):
        table = jnp.where(chosen, value, 0.0).astype(jnp.bfloat16)
        meta.append(lax.dot_general(table, marks, NT, preferred_element_type=jnp.float32).astype(jnp.bfloat16))
    if meta_ref is None:
        tail = jnp.concatenate([m.reshape(owners, 1, LANES) for m in meta] * 4, axis=1)
        out_ref[:, panels_ref.shape[0] * length :, :] = tail
    else:
        for k in range(2):
            meta_ref[k] = meta[k]


META_ROWS = 8


def pack(owners, slots, ranks, tiles, offsets, panels):
    components = panels.shape[0]
    vmem = pl.BlockSpec(memory_space=pltpu.VMEM)
    kernel = functools.partial(pack_kernel, owners, slots, ranks)
    if ranks % 16 == 0:
        return pl.pallas_call(
            kernel,
            out_shape=jax.ShapeDtypeStruct((owners, components * ranks + META_ROWS, LANES), jnp.bfloat16),
            in_specs=[vmem] * 3,
            out_specs=vmem,
            name="pack",
        )(tiles, offsets, panels)
    body, meta = pl.pallas_call(
        kernel,
        out_shape=(
            jax.ShapeDtypeStruct((1, components * owners * ranks, LANES), jnp.bfloat16),
            jax.ShapeDtypeStruct((2, owners, LANES), jnp.bfloat16),
        ),
        in_specs=[vmem] * 3,
        out_specs=(vmem, vmem),
        name="pack",
    )(tiles, offsets, panels)
    body = body.reshape(components, owners, ranks, LANES).transpose(1, 0, 2, 3)
    body = body.reshape(owners, components * ranks, LANES)
    return jnp.concatenate([body, meta.transpose(1, 0, 2)], axis=1)


def unpack(owners, ranks, components, arrived):
    if ranks % 16 == 0:
        return (arrived,)
    body = arrived[:, : components * ranks]
    meta = arrived[:, components * ranks :].transpose(1, 0, 2)
    body = body.reshape(owners, components, ranks, LANES).transpose(1, 0, 2, 3)
    return body.reshape(1, components * owners * ranks, LANES), meta


def planes_for(side, halo, nx):
    plan = []
    for field in range(FIELDS):
        count = halo if field < 3 or (side > 0 and field in (6, 7)) else halo - 1
        plan.append((field, nx - count if side > 0 else 0, count))
    return plan


def prepare_kernel(halo, merged, *refs):
    disp, prev, lam, mu, buoy, fields, up, down = refs[:8]
    edges, sem = refs[8:-1], refs[-1]
    nx, ny, nz = lam.shape
    copies = [
        pltpu.make_async_copy(disp.at[0], fields.at[pl.ds(0, 3)], sem.at[0]),
        pltpu.make_async_copy(prev.at[0], fields.at[pl.ds(3, 3)], sem.at[1]),
        pltpu.make_async_copy(lam, fields.at[6], sem.at[2]),
        pltpu.make_async_copy(mu, fields.at[7], sem.at[3]),
        pltpu.make_async_copy(buoy, fields.at[8], sem.at[4]),
    ]
    for copy in copies:
        copy.start()
    gy = lax.axis_index("gy")
    done = 0
    for side, target in ((1, up), (-1, down)):
        at = 0
        for field, first, count in planes_for(side, halo, nx):
            while done < len(copies) and field >= (0, 3, 6, 7, 8)[done]:
                copies[done].wait()
                done += 1
            target[at : at + count] = fields[field, first : first + count]
            at += count
    high, low = pl.ds(ny - halo, halo), pl.ds(0, halo)
    if merged:

        @pl.when(gy == 0)
        def _():
            edges[0][...] = fields[:, :, high, :]

        @pl.when(gy != 0)
        def _():
            edges[0][...] = fields[:, :, low, :]
    else:
        edges[0][...] = fields[:, :, high, :]
        edges[1][...] = fields[:, :, low, :]


def prepare(halo, merged, disp, prev, lam, mu, buoy):
    nx, ny, nz = lam.shape
    vmem, anywhere = pl.BlockSpec(memory_space=pltpu.VMEM), pl.BlockSpec(memory_space=pl.ANY)
    totals = [sum(count for _, _, count in planes_for(side, halo, nx)) for side in (1, -1)]
    shapes = [(FIELDS, nx, ny, nz)] + [(total, ny, nz) for total in totals]
    shapes += [(FIELDS, nx, halo, nz)] * (1 if merged else 2)
    return pl.pallas_call(
        functools.partial(prepare_kernel, halo, merged),
        out_shape=[jax.ShapeDtypeStruct(shape, jnp.float32) for shape in shapes],
        in_specs=[anywhere] * 5,
        out_specs=[vmem] * len(shapes),
        scratch_shapes=[pltpu.SemaphoreType.DMA((5,))],
        name="prepare",
    )(disp, prev, lam, mu, buoy)


def shifted_up(value, dim):
    return pltpu.roll(value, value.shape[dim] - 1, dim)


def stencil_kernel(halo, merged, *refs):
    fields, x_low, x_high = refs[:3]
    sides = refs[3:9] if not merged else refs[3:6] * 2
    out_ref, strain_ref = refs[-7:-5]
    wave, first, second, scale = refs[-5:-1]
    _, nx, ny, nz = fields.shape
    tall = ny + 2 * PAD
    gy = lax.axis_index("gy")
    own_x, own_y = pl.ds(halo, nx), pl.ds(PAD, ny)
    lows, highs = pl.ds(0, halo), pl.ds(halo + nx, halo)

    targets = [wave.at[0, i] for i in range(3)] + [wave.at[1, i] for i in range(3)] + [first, second, scale]
    low_at = high_at = 0
    for f, target in enumerate(targets):

        def put(xs, ys, value, f=f, target=target):
            target[xs, ys, :] = value * (TIME_STEP * TIME_STEP) if f == 8 else value

        put(own_x, own_y, fields[f])
        _, _, count = planes_for(1, halo, nx)[f]
        put(pl.ds(halo - count, count), own_y, x_low[low_at : low_at + count])
        low_at += count
        _, _, count = planes_for(-1, halo, nx)[f]
        put(pl.ds(halo + nx, count), own_y, x_high[high_at : high_at + count])
        high_at += count
        for s, ys in ((0, pl.ds(PAD - halo, halo)), (1, pl.ds(PAD + ny, halo))):
            middle, low, high = [r[f] for r in sides[3 * s : 3 * s + 3]]
            if merged:
                here = gy == (1 - s)
                middle, low, high = [jnp.where(here, v, 0.0) for v in (middle, low, high)]
            put(own_x, ys, middle)
            put(lows, ys, low)
            put(highs, ys, high)

    lane = iota((tall, nz), 1)
    not_last, not_first = lane < nz - 1, lane > 0

    def fields(cur, x):
        base = [wave[cur, i, x] for i in range(3)]
        nxt = [wave[cur, i, x + 1] for i in range(3)]
        dx = [n - b for n, b in zip(nxt, base)]
        dy = [shifted_up(b, 0) - b for b in base]
        dz = [jnp.where(not_last, shifted_up(b, 1), 0.0) - b for b in base]
        normal = [dx[0], dy[1], dz[2]]
        twice = [dy[0] + dx[1], dz[0] + dx[2], dz[1] + dy[2]]
        m = second[x]
        volume = first[x] * (normal[0] + normal[1] + normal[2])
        m2 = m + m
        stress = [volume + m2 * e for e in normal] + [m * e for e in twice]
        return base, normal, twice, stress

    def back_y(v):
        return v - pltpu.roll(v, 1, 0)

    def back_z(v):
        return v - jnp.where(not_first, pltpu.roll(v, 1, 1), 0.0)

    def plane(step, cur, own, x, carry):
        base, normal, twice, stress = fields(cur, x)
        if own:
            rows = pl.ds(pl.multiple_of(step * nx * ny + (x - halo) * ny, ny), ny)
            for e, value in enumerate(normal + [0.5 * t for t in twice]):
                strain_ref[rows, e * nz : (e + 1) * nz] = value[PAD : PAD + ny].astype(jnp.bfloat16)
        xx, yy, zz, xy, xz, yz = stress
        forces = [
            (xx - carry[0]) + back_y(xy) + back_z(xz),
            (xy - carry[1]) + back_y(yy) + back_z(yz),
            (xz - carry[2]) + back_y(yz) + back_z(zz),
        ]
        for i in range(3):
            value = 2.0 * base[i] - wave[1 - cur, i, x] + scale[x] * forces[i]
            if step == STEPS - 1:
                out_ref[0, i, x - halo] = value[PAD : PAD + ny]
            else:
                wave[1 - cur, i, x] = value
        return xx, xy, xz

    for step in range(STEPS):
        cur = step % 2
        reach = STEPS - 1 - step
        begin, end = halo - reach, halo + nx + reach
        stress = fields(cur, begin - 1)[3]
        carry = (stress[0], stress[3], stress[4])
        for lo, hi, own in ((begin, halo, False), (halo, halo + nx, True), (halo + nx, end, False)):
            if hi > lo:
                carry = lax.fori_loop(lo, hi, functools.partial(plane, step, cur, own), carry)


def stencil(halo, merged, fields, x_low, x_high, sides):
    _, nx, ny, nz = fields.shape
    tall, wide = ny + 2 * PAD, nx + 2 * halo
    vmem = pl.BlockSpec(memory_space=pltpu.VMEM)
    operands = (fields, x_low, x_high, *sides)
    return pl.pallas_call(
        functools.partial(stencil_kernel, halo, merged),
        out_shape=(
            jax.ShapeDtypeStruct((1, 3, nx, ny, nz), jnp.float32),
            jax.ShapeDtypeStruct((STEPS * nx * ny, 6 * nz), jnp.bfloat16),
        ),
        in_specs=[vmem] * len(operands),
        out_specs=(vmem, vmem),
        scratch_shapes=[pltpu.VMEM((2, 3, wide, tall, nz), jnp.float32)]
        + [pltpu.VMEM((wide, tall, nz), jnp.float32)] * 3
        + [pltpu.SMEM((1,), jnp.int32)],
        compiler_params=pltpu.CompilerParams(vmem_limit_bytes=40 << 20),
        cost_estimate=pl.CostEstimate(flops=10**10, transcendentals=10**8, bytes_accessed=10**8),
        name="stencil",
    )(*operands)


def response_kernel(owners, ranks, records, strain_ref, column_ref, *refs):
    points = column_ref.shape[1]
    sent = owners * ranks
    group = LANES // ranks
    columns = strain_ref.shape[0] // STEPS
    total, out_ref = None, refs[-1]
    friendly = ranks % 16 == 0
    for half in range(2):
        pan = refs[half if friendly else 2 * half]
        length = sent // pan.shape[0]
        rows = []
        for k in range(2):
            table = pan[:, 6 * length + k, :] if friendly else refs[2 * half + 1][k]
            table = table.astype(jnp.float32)
            parts = [
                jnp.sum(table[g * group : (g + 1) * group], axis=0, keepdims=True) for g in range(owners // group)
            ]
            rows.append(jnp.concatenate(parts, axis=1))
        slot, record = rows
        owner = iota((1, sent), 1) // ranks
        spread = (iota((points, sent), 0) == slot.astype(jnp.int32)).astype(jnp.bfloat16)
        table = jnp.broadcast_to(column_ref[...].astype(jnp.float32), (8, points)).astype(jnp.bfloat16)
        column = jnp.dot(table, spread, preferred_element_type=jnp.float32)[:1].astype(jnp.int32)
        grid = None
        for i in range(3):
            right = jnp.concatenate(
                [pan[:, (2 * i + k) * length : (2 * i + k + 1) * length, :].reshape(sent, LANES) for k in range(2)],
                axis=1,
            )
            left = strain_ref[:, 2 * i * LANES : (2 * i + 2) * LANES]
            term = lax.dot_general(left, right, NT, preferred_element_type=jnp.float32)
            grid = term if grid is None else grid + term
        mark = iota((columns, sent), 0) == column
        reply = [
            jnp.sum(jnp.where(mark, grid[m * columns : (m + 1) * columns], 0.0), axis=0, keepdims=True)
            for m in range(STEPS)
        ]
        record = record.astype(jnp.int32)
        offset = record % STEPS
        delayed = []
        for n in range(STEPS):
            value = jnp.where(offset == n, reply[0], 0.0)
            for m in range(1, n + 1):
                value = value + jnp.where(offset == n - m, reply[m], 0.0)
            delayed.append(value)
        delayed = jnp.concatenate(delayed + [jnp.zeros((8 - STEPS, sent), jnp.float32)], axis=0)
        key = owner * records + record // STEPS
        gather = (iota((owners * records, sent), 0) == key).astype(jnp.float32)
        part = lax.dot_general(
            delayed, gather, NT, preferred_element_type=jnp.float32, precision=lax.Precision.HIGHEST
        )
        total = part if total is None else total + part
    out_ref[...] = total[:STEPS]


def respond(owners, ranks, records, strain, columns, halves):
    vmem = pl.BlockSpec(memory_space=pltpu.VMEM)
    operands = (strain, columns, *halves[0], *halves[1])
    return pl.pallas_call(
        functools.partial(response_kernel, owners, ranks, records),
        out_shape=jax.ShapeDtypeStruct((STEPS, owners * records), jnp.float32),
        in_specs=[vmem] * len(operands),
        out_specs=vmem,
        compiler_params=pltpu.CompilerParams(vmem_limit_bytes=40 << 20),
        name="respond",
    )(*operands)


def shift_pairs(nx, ny, dx, dy):
    return [
        (i * ny + j, (i + dx) * ny + j + dy)
        for i in range(nx)
        for j in range(ny)
        if 0 <= i + dx < nx and 0 <= j + dy < ny
    ]


def owner_sum(value, owners):
    if owners & (owners - 1):
        return lax.psum(value, OWNERS_AXES)
    bit = 1
    while bit < owners:
        value = value + lax.ppermute(value, OWNERS_AXES, [(i, i ^ bit) for i in range(owners)])
        bit *= 2
    return value


def body(displacement, previous, first_lame, shear_modulus, buoyancy, tile_column, rupture_tiles, slip_offsets, slip_panels):
    gxs, gys = lax.axis_size("gx"), lax.axis_size("gy")
    owners = gxs * gys
    nx, ny, nz = shear_modulus.shape
    halo = STEPS
    slots = tile_column.shape[0]
    records, listed = rupture_tiles.shape
    entries = records * listed
    ranks = entries // owners
    components = slip_panels.shape[2]

    merged = gys == 2
    fields, upward, downward, *edges = prepare(
        halo, merged, displacement, previous, first_lame, shear_modulus, buoyancy
    )

    def send(value, dx, dy):
        pairs = shift_pairs(gxs, gys, dx, dy)
        if merged and dy:
            pairs = pairs + shift_pairs(gxs, gys, dx, -dy)
        return lax.ppermute(value, OWNERS_AXES, pairs)

    if merged:
        sides = [send(edges[0], dx, 1) for dx in (0, 1, -1)]
    else:
        sides = [send(edge, dx, dy) for edge, dy in zip(edges, (1, -1)) for dx in (0, 1, -1)]
    x_low, x_high = send(upward, 1, 0), send(downward, -1, 0)

    sides[0], slip_panels = lax.optimization_barrier((sides[0], slip_panels))
    panels = slip_panels.reshape(entries, components, nz).transpose(1, 0, 2)
    payload = pack(owners, slots, ranks, rupture_tiles, slip_offsets, panels)
    arrived = lax.all_to_all(payload, OWNERS_AXES, split_axis=0, concat_axis=0, tiled=True)
    final, strain = stencil(halo, merged, fields, x_low, x_high, sides)
    arrived, strain = lax.optimization_barrier((arrived, strain))
    other = lax.ppermute(arrived, "comp", [(0, 1), (1, 0)])
    halves = [unpack(owners, ranks, components, v) for v in (arrived, other)]
    partial = respond(owners, ranks, records, strain, tile_column.reshape(1, slots), halves)
    summed = owner_sum(partial, owners)
    mine = lax.dynamic_slice_in_dim(summed, owner_index() * records, records, axis=1)
    return final, mine.T[None]


def solution(mesh):
    in_specs = (
        P("comp", None, ("site", "gx"), "gy", None),
        P("comp", None, ("site", "gx"), "gy", None),
        P(("site", "gx"), "gy", None),
        P(("site", "gx"), "gy", None),
        P(("site", "gx"), "gy", None),
        P(("site", "gx", "gy")),
        P(("site", "gx", "gy"), None),
        P(("site", "gx", "gy"), None),
        P(("site", "gx", "gy"), None, None, None),
    )
    out_specs = (P("comp", None, ("site", "gx"), "gy", None), P("comp", ("site", "gx", "gy"), None))
    return jax.shard_map(body, mesh=mesh, in_specs=in_specs, out_specs=out_specs, check_vma=False)
```

```python
import functools

import jax
import jax.numpy as jnp
from jax import lax
from jax.experimental import pallas as pl
from jax.experimental.pallas import tpu as pltpu
from jax.sharding import PartitionSpec as P

STEPS = 4
TIME_STEP = 0.12
LANES = 128
PAD = 8
OWNERS_AXES = ("gx", "gy")
FIELDS = 9
NT = (((1,), (1,)), ((), ()))


def iota(shape, dim):
    return lax.broadcasted_iota(jnp.int32, shape, dim)


def owner_index():
    return lax.axis_index("gx") * lax.axis_size("gy") + lax.axis_index("gy")


def pack_kernel(owners, slots, ranks, tiles_ref, offsets_ref, panels_ref, out_ref, meta_ref=None):
    rows, cols = tiles_ref.shape
    entries = rows * cols
    core = lax.axis_index("comp")
    me = owner_index()
    tiles = tiles_ref[...]
    shift = slots.bit_length() - 1
    fields = jnp.concatenate([tiles >> shift, tiles & (slots - 1), offsets_ref[...]], axis=0)
    spread = (iota((cols, entries), 1) % cols == iota((cols, entries), 0)).astype(jnp.bfloat16)
    wide = jnp.dot(fields.astype(jnp.float32).astype(jnp.bfloat16), spread, preferred_element_type=jnp.float32)
    lane_row = iota((rows, entries), 1) // cols
    keep = lane_row == iota((rows, entries), 0)
    source, slot, offset = [
        jnp.sum(jnp.where(keep, wide[i * rows : (i + 1) * rows], 0.0), axis=0, keepdims=True) for i in range(3)
    ]
    record = (iota((1, entries), 1) // cols).astype(jnp.float32) * STEPS + offset
    chosen = source == iota((owners, entries), 0).astype(jnp.float32)
    before = (iota((entries, entries), 0) < iota((entries, entries), 1)).astype(jnp.bfloat16)
    counts = jnp.dot(chosen.astype(jnp.bfloat16), before, preferred_element_type=jnp.float32)
    rank = jnp.sum(jnp.where(chosen, counts, 0.0), axis=0, keepdims=True).astype(jnp.int32) - core * ranks
    mine = (rank >= 0) & (rank < ranks)
    place = jnp.where(mine, source.astype(jnp.int32) * ranks + rank, -1)
    sent = owners * ranks
    select = (iota((sent, entries), 0) == place).astype(jnp.bfloat16)
    blocks = out_ref.shape[0]
    length = sent // blocks
    for i in range(panels_ref.shape[0]):
        part = jnp.dot(select, panels_ref[i], preferred_element_type=jnp.float32).astype(jnp.bfloat16)
        out_ref[:, i * length : (i + 1) * length, :] = part.reshape(blocks, length, LANES)
    group = LANES // ranks
    lane = jnp.where(mine, rank + ranks * (me % group), -1)
    marks = (iota((LANES, entries), 0) == lane).astype(jnp.bfloat16)
    meta = []
    for value in (slot, record):
        table = jnp.where(chosen, value, 0.0).astype(jnp.bfloat16)
        meta.append(lax.dot_general(table, marks, NT, preferred_element_type=jnp.float32).astype(jnp.bfloat16))
    if meta_ref is None:
        tail = jnp.concatenate([m.reshape(owners, 1, LANES) for m in meta] * 4, axis=1)
        out_ref[:, panels_ref.shape[0] * length :, :] = tail
    else:
        for k in range(2):
            meta_ref[k] = meta[k]


META_ROWS = 8


def pack(owners, slots, ranks, tiles, offsets, panels):
    components = panels.shape[0]
    vmem = pl.BlockSpec(memory_space=pltpu.VMEM)
    kernel = functools.partial(pack_kernel, owners, slots, ranks)
    if ranks % 16 == 0:
        return pl.pallas_call(
            kernel,
            out_shape=jax.ShapeDtypeStruct((owners, components * ranks + META_ROWS, LANES), jnp.bfloat16),
            in_specs=[vmem] * 3,
            out_specs=vmem,
            name="pack",
        )(tiles, offsets, panels)
    body, meta = pl.pallas_call(
        kernel,
        out_shape=(
            jax.ShapeDtypeStruct((1, components * owners * ranks, LANES), jnp.bfloat16),
            jax.ShapeDtypeStruct((2, owners, LANES), jnp.bfloat16),
        ),
        in_specs=[vmem] * 3,
        out_specs=(vmem, vmem),
        name="pack",
    )(tiles, offsets, panels)
    body = body.reshape(components, owners, ranks, LANES).transpose(1, 0, 2, 3)
    body = body.reshape(owners, components * ranks, LANES)
    return jnp.concatenate([body, meta.transpose(1, 0, 2)], axis=1)


def unpack(owners, ranks, components, arrived):
    if ranks % 16 == 0:
        return (arrived,)
    body = arrived[:, : components * ranks]
    meta = arrived[:, components * ranks :].transpose(1, 0, 2)
    body = body.reshape(owners, components, ranks, LANES).transpose(1, 0, 2, 3)
    return body.reshape(1, components * owners * ranks, LANES), meta


def planes_for(field, side, halo):
    return halo if field < 3 or (side > 0 and field in (6, 7)) else halo - 1


def coded_planes(side, halo):
    return sum(planes_for(f, side, halo) + (f < 6) for f in range(FIELDS))


def encode(side, halo, nx, read, write):
    at = 0
    for field in range(FIELDS):
        near = None
        for k in range(planes_for(field, side, halo)):
            value = read(field, nx - 1 - k if side > 0 else k)
            if field >= 6:
                parts = [value.astype(jnp.bfloat16)]
            elif near is None:
                high = value.astype(jnp.bfloat16)
                low = (value - high.astype(jnp.float32)).astype(jnp.bfloat16)
                near = high.astype(jnp.float32) + low.astype(jnp.float32)
                parts = [high, low]
            else:
                step = (value - near).astype(jnp.bfloat16)
                near = near + step.astype(jnp.float32)
                parts = [step]
            for part in parts:
                write(at, part)
                at += 1


def decode(side, halo, nx, read, write):
    at = 0
    for field in range(FIELDS):
        near = None
        for k in range(planes_for(field, side, halo)):
            value = read(at).astype(jnp.float32)
            at += 1
            if field < 6:
                if near is None:
                    value = value + read(at).astype(jnp.float32)
                    at += 1
                else:
                    value = near + value
                near = value
            write(field, halo - 1 - k if side > 0 else halo + nx + k, value)


def prepare_kernel(halo, merged, *refs):
    disp, prev, lam, mu, buoy, up, down = refs[:7]
    edges, fields, sem = refs[7:-2], refs[-2], refs[-1]
    nx, ny, nz = lam.shape
    copies = [
        pltpu.make_async_copy(disp.at[0], fields.at[pl.ds(0, 3)], sem.at[0]),
        pltpu.make_async_copy(prev.at[0], fields.at[pl.ds(3, 3)], sem.at[1]),
        pltpu.make_async_copy(lam, fields.at[6], sem.at[2]),
        pltpu.make_async_copy(mu, fields.at[7], sem.at[3]),
        pltpu.make_async_copy(buoy, fields.at[8], sem.at[4]),
    ]
    for copy in copies:
        copy.start()
    for copy in copies:
        copy.wait()

    def coded(side, rows, target):
        def write(at, value):
            target[at] = value

        encode(side, halo, nx, lambda f, x: fields[f, x, rows, :], write)

    every, high, low = pl.ds(0, ny), pl.ds(ny - halo, halo), pl.ds(0, halo)
    coded(1, every, up)
    coded(-1, every, down)

    def edge(rows, targets):
        targets[0][...] = fields[:, :, rows, :]
        coded(1, rows, targets[1])
        coded(-1, rows, targets[2])

    if merged:
        gy = lax.axis_index("gy")
        pl.when(gy == 0)(lambda: edge(high, edges))
        pl.when(gy != 0)(lambda: edge(low, edges))
    else:
        edge(high, edges[:3])
        edge(low, edges[3:])


def prepare(halo, merged, disp, prev, lam, mu, buoy):
    nx, ny, nz = lam.shape
    vmem, anywhere = pl.BlockSpec(memory_space=pltpu.VMEM), pl.BlockSpec(memory_space=pl.ANY)
    counts = [coded_planes(side, halo) for side in (1, -1)]
    shapes = [jax.ShapeDtypeStruct((count, ny, nz), jnp.bfloat16) for count in counts]
    edge = [jax.ShapeDtypeStruct((FIELDS, nx, halo, nz), jnp.float32)]
    edge += [jax.ShapeDtypeStruct((count, halo, nz), jnp.bfloat16) for count in counts]
    shapes += edge if merged else edge * 2
    return pl.pallas_call(
        functools.partial(prepare_kernel, halo, merged),
        out_shape=shapes,
        in_specs=[anywhere] * 5,
        out_specs=[vmem] * len(shapes),
        scratch_shapes=[pltpu.VMEM((FIELDS, nx, ny, nz), jnp.float32), pltpu.SemaphoreType.DMA((5,))],
        name="prepare",
    )(disp, prev, lam, mu, buoy)


def shifted_up(value, dim):
    return pltpu.roll(value, value.shape[dim] - 1, dim)


def stencil_kernel(halo, merged, *refs):
    disp, prev, lam, mu, buoy, x_low, x_high = refs[:7]
    sides = refs[7:13] if not merged else refs[7:10] * 2
    out_ref, strain_ref = refs[-7:-5]
    wave, first, second, scale = refs[-5:-1]
    nx, ny, nz = lam.shape
    tall = ny + 2 * PAD
    gy = lax.axis_index("gy")
    own_x, own_y = pl.ds(halo, nx), pl.ds(PAD, ny)
    targets = [wave.at[0, i] for i in range(3)] + [wave.at[1, i] for i in range(3)] + [first, second, scale]

    def put(field, xs, ys, value):
        targets[field][xs, ys, :] = value * (TIME_STEP * TIME_STEP) if field == 8 else value

    owns = [disp[0, i] for i in range(3)] + [prev[0, i] for i in range(3)] + [lam[...], mu[...], buoy[...]]
    for f, own in enumerate(owns):
        put(f, own_x, own_y, own)
    decode(1, halo, nx, lambda at: x_low[at], lambda f, x, v: put(f, x, own_y, v))
    decode(-1, halo, nx, lambda at: x_high[at], lambda f, x, v: put(f, x, own_y, v))
    for s, ys in ((0, pl.ds(PAD - halo, halo)), (1, pl.ds(PAD + ny, halo))):
        middle, low, high = sides[3 * s : 3 * s + 3]

        def only(value, s=s):
            return jnp.where(gy == (1 - s), value, 0.0) if merged else value

        for f in range(FIELDS):
            put(f, own_x, ys, only(middle[f]))
        decode(1, halo, nx, lambda at: low[at], lambda f, x, v: put(f, x, ys, only(v)))
        decode(-1, halo, nx, lambda at: high[at], lambda f, x, v: put(f, x, ys, only(v)))

    lane = iota((tall, nz), 1)
    not_last, not_first = lane < nz - 1, lane > 0

    def fields(cur, x):
        base = [wave[cur, i, x] for i in range(3)]
        nxt = [wave[cur, i, x + 1] for i in range(3)]
        dx = [n - b for n, b in zip(nxt, base)]
        dy = [shifted_up(b, 0) - b for b in base]
        dz = [jnp.where(not_last, shifted_up(b, 1), 0.0) - b for b in base]
        normal = [dx[0], dy[1], dz[2]]
        twice = [dy[0] + dx[1], dz[0] + dx[2], dz[1] + dy[2]]
        m = second[x]
        volume = first[x] * (normal[0] + normal[1] + normal[2])
        m2 = m + m
        stress = [volume + m2 * e for e in normal] + [m * e for e in twice]
        return base, normal, twice, stress

    def back_y(v):
        return v - pltpu.roll(v, 1, 0)

    def back_z(v):
        return v - jnp.where(not_first, pltpu.roll(v, 1, 1), 0.0)

    def plane(step, cur, own, x, carry):
        base, normal, twice, stress = fields(cur, x)
        if own:
            rows = pl.ds(pl.multiple_of(step * nx * ny + (x - halo) * ny, ny), ny)
            for e, value in enumerate(normal + [0.5 * t for t in twice]):
                strain_ref[rows, e * nz : (e + 1) * nz] = value[PAD : PAD + ny].astype(jnp.bfloat16)
        xx, yy, zz, xy, xz, yz = stress
        forces = [
            (xx - carry[0]) + back_y(xy) + back_z(xz),
            (xy - carry[1]) + back_y(yy) + back_z(yz),
            (xz - carry[2]) + back_y(yz) + back_z(zz),
        ]
        for i in range(3):
            value = 2.0 * base[i] - wave[1 - cur, i, x] + scale[x] * forces[i]
            if step == STEPS - 1:
                out_ref[0, i, x - halo] = value[PAD : PAD + ny]
            else:
                wave[1 - cur, i, x] = value
        return xx, xy, xz

    for step in range(STEPS):
        cur = step % 2
        reach = STEPS - 1 - step
        begin, end = halo - reach, halo + nx + reach
        stress = fields(cur, begin - 1)[3]
        carry = (stress[0], stress[3], stress[4])
        for lo, hi, own in ((begin, halo, False), (halo, halo + nx, True), (halo + nx, end, False)):
            if hi > lo:
                carry = lax.fori_loop(lo, hi, functools.partial(plane, step, cur, own), carry)


def stencil(halo, merged, disp, prev, lam, mu, buoy, x_low, x_high, sides):
    nx, ny, nz = lam.shape
    tall, wide = ny + 2 * PAD, nx + 2 * halo
    vmem = pl.BlockSpec(memory_space=pltpu.VMEM)
    operands = (disp, prev, lam, mu, buoy, x_low, x_high, *sides)
    return pl.pallas_call(
        functools.partial(stencil_kernel, halo, merged),
        out_shape=(
            jax.ShapeDtypeStruct((1, 3, nx, ny, nz), jnp.float32),
            jax.ShapeDtypeStruct((STEPS * nx * ny, 6 * nz), jnp.bfloat16),
        ),
        in_specs=[vmem] * len(operands),
        out_specs=(vmem, vmem),
        scratch_shapes=[pltpu.VMEM((2, 3, wide, tall, nz), jnp.float32)]
        + [pltpu.VMEM((wide, tall, nz), jnp.float32)] * 3
        + [pltpu.SMEM((1,), jnp.int32)],
        compiler_params=pltpu.CompilerParams(vmem_limit_bytes=40 << 20),
        cost_estimate=pl.CostEstimate(flops=10**10, transcendentals=10**8, bytes_accessed=10**8),
        name="stencil",
    )(*operands)


def response_kernel(owners, ranks, records, strain_ref, column_ref, *refs):
    points = column_ref.shape[1]
    sent = owners * ranks
    group = LANES // ranks
    columns = strain_ref.shape[0] // STEPS
    total, out_ref = None, refs[-1]
    friendly = ranks % 16 == 0
    for half in range(2):
        pan = refs[half if friendly else 2 * half]
        length = sent // pan.shape[0]
        rows = []
        for k in range(2):
            table = pan[:, 6 * length + k, :] if friendly else refs[2 * half + 1][k]
            table = table.astype(jnp.float32)
            parts = [
                jnp.sum(table[g * group : (g + 1) * group], axis=0, keepdims=True) for g in range(owners // group)
            ]
            rows.append(jnp.concatenate(parts, axis=1))
        slot, record = rows
        owner = iota((1, sent), 1) // ranks
        spread = (iota((points, sent), 0) == slot.astype(jnp.int32)).astype(jnp.bfloat16)
        table = jnp.broadcast_to(column_ref[...].astype(jnp.float32), (8, points)).astype(jnp.bfloat16)
        column = jnp.dot(table, spread, preferred_element_type=jnp.float32)[:1].astype(jnp.int32)
        grid = None
        for i in range(3):
            right = jnp.concatenate(
                [pan[:, (2 * i + k) * length : (2 * i + k + 1) * length, :].reshape(sent, LANES) for k in range(2)],
                axis=1,
            )
            left = strain_ref[:, 2 * i * LANES : (2 * i + 2) * LANES]
            term = lax.dot_general(left, right, NT, preferred_element_type=jnp.float32)
            grid = term if grid is None else grid + term
        mark = iota((columns, sent), 0) == column
        reply = [
            jnp.sum(jnp.where(mark, grid[m * columns : (m + 1) * columns], 0.0), axis=0, keepdims=True)
            for m in range(STEPS)
        ]
        record = record.astype(jnp.int32)
        offset = record % STEPS
        delayed = []
        for n in range(STEPS):
            value = jnp.where(offset == n, reply[0], 0.0)
            for m in range(1, n + 1):
                value = value + jnp.where(offset == n - m, reply[m], 0.0)
            delayed.append(value)
        delayed = jnp.concatenate(delayed + [jnp.zeros((8 - STEPS, sent), jnp.float32)], axis=0)
        key = owner * records + record // STEPS
        gather = (iota((owners * records, sent), 0) == key).astype(jnp.float32)
        part = lax.dot_general(
            delayed, gather, NT, preferred_element_type=jnp.float32, precision=lax.Precision.HIGHEST
        )
        total = part if total is None else total + part
    out_ref[...] = total[:STEPS]


def respond(owners, ranks, records, strain, columns, halves):
    vmem = pl.BlockSpec(memory_space=pltpu.VMEM)
    operands = (strain, columns, *halves[0], *halves[1])
    return pl.pallas_call(
        functools.partial(response_kernel, owners, ranks, records),
        out_shape=jax.ShapeDtypeStruct((STEPS, owners * records), jnp.float32),
        in_specs=[vmem] * len(operands),
        out_specs=vmem,
        compiler_params=pltpu.CompilerParams(vmem_limit_bytes=40 << 20),
        name="respond",
    )(*operands)


def shift_pairs(nx, ny, dx, dy):
    return [
        (i * ny + j, (i + dx) * ny + j + dy)
        for i in range(nx)
        for j in range(ny)
        if 0 <= i + dx < nx and 0 <= j + dy < ny
    ]


def owner_sum(value, owners):
    if owners & (owners - 1):
        return lax.psum(value, OWNERS_AXES)
    bit = 1
    while bit < owners:
        value = value + lax.ppermute(value, OWNERS_AXES, [(i, i ^ bit) for i in range(owners)])
        bit *= 2
    return value


def body(displacement, previous, first_lame, shear_modulus, buoyancy, tile_column, rupture_tiles, slip_offsets, slip_panels):
    gxs, gys = lax.axis_size("gx"), lax.axis_size("gy")
    owners = gxs * gys
    nx, ny, nz = shear_modulus.shape
    halo = STEPS
    slots = tile_column.shape[0]
    records, listed = rupture_tiles.shape
    entries = records * listed
    ranks = entries // owners
    components = slip_panels.shape[2]

    merged = gys == 2
    upward, downward, *edges = prepare(
        halo, merged, displacement, previous, first_lame, shear_modulus, buoyancy
    )

    def send(value, dx, dy):
        pairs = shift_pairs(gxs, gys, dx, dy)
        if merged and dy:
            pairs = pairs + shift_pairs(gxs, gys, dx, -dy)
        return lax.ppermute(value, OWNERS_AXES, pairs)

    ways = [(0, 1), (1, 1), (-1, 1)] + ([] if merged else [(0, -1), (1, -1), (-1, -1)])
    sides = [send(edge, dx, dy) for edge, (dx, dy) in zip(edges, ways)]
    x_low, x_high = send(upward, 1, 0), send(downward, -1, 0)

    sides[0], slip_panels = lax.optimization_barrier((sides[0], slip_panels))
    panels = slip_panels.reshape(entries, components, nz).transpose(1, 0, 2)
    payload = pack(owners, slots, ranks, rupture_tiles, slip_offsets, panels)
    arrived = lax.all_to_all(payload, OWNERS_AXES, split_axis=0, concat_axis=0, tiled=True)
    final, strain = stencil(
        halo, merged, displacement, previous, first_lame, shear_modulus, buoyancy, x_low, x_high, sides
    )
    arrived, strain = lax.optimization_barrier((arrived, strain))
    other = lax.ppermute(arrived, "comp", [(0, 1), (1, 0)])
    halves = [unpack(owners, ranks, components, v) for v in (arrived, other)]
    partial = respond(owners, ranks, records, strain, tile_column.reshape(1, slots), halves)
    summed = owner_sum(partial, owners)
    mine = lax.dynamic_slice_in_dim(summed, owner_index() * records, records, axis=1)
    return final, mine.T[None]


def solution(mesh):
    in_specs = (
        P("comp", None, ("site", "gx"), "gy", None),
        P("comp", None, ("site", "gx"), "gy", None),
        P(("site", "gx"), "gy", None),
        P(("site", "gx"), "gy", None),
        P(("site", "gx"), "gy", None),
        P(("site", "gx", "gy")),
        P(("site", "gx", "gy"), None),
        P(("site", "gx", "gy"), None),
        P(("site", "gx", "gy"), None, None, None),
    )
    out_specs = (P("comp", None, ("site", "gx"), "gy", None), P("comp", ("site", "gx", "gy"), None))
    return jax.shard_map(body, mesh=mesh, in_specs=in_specs, out_specs=out_specs, check_vma=False)
```

```python
import functools

import jax
import jax.numpy as jnp
from jax import lax
from jax.experimental import pallas as pl
from jax.experimental.pallas import tpu as pltpu
from jax.sharding import PartitionSpec as P

STEPS = 4
TIME_STEP = 0.12
LANES = 128
PAD = 8
OWNERS_AXES = ("gx", "gy")
FIELDS = 9
NT = (((1,), (1,)), ((), ()))


def iota(shape, dim):
    return lax.broadcasted_iota(jnp.int32, shape, dim)


def owner_index():
    return lax.axis_index("gx") * lax.axis_size("gy") + lax.axis_index("gy")


def pack_kernel(owners, slots, ranks, tiles_ref, offsets_ref, panels_ref, out_ref, meta_ref=None):
    rows, cols = tiles_ref.shape
    entries = rows * cols
    core = lax.axis_index("comp")
    me = owner_index()
    tiles = tiles_ref[...]
    shift = slots.bit_length() - 1
    fields = jnp.concatenate([tiles >> shift, tiles & (slots - 1), offsets_ref[...]], axis=0)
    spread = (iota((cols, entries), 1) % cols == iota((cols, entries), 0)).astype(jnp.bfloat16)
    wide = jnp.dot(fields.astype(jnp.float32).astype(jnp.bfloat16), spread, preferred_element_type=jnp.float32)
    lane_row = iota((rows, entries), 1) // cols
    keep = lane_row == iota((rows, entries), 0)
    source, slot, offset = [
        jnp.sum(jnp.where(keep, wide[i * rows : (i + 1) * rows], 0.0), axis=0, keepdims=True) for i in range(3)
    ]
    record = (iota((1, entries), 1) // cols).astype(jnp.float32) * STEPS + offset
    chosen = source == iota((owners, entries), 0).astype(jnp.float32)
    before = (iota((entries, entries), 0) < iota((entries, entries), 1)).astype(jnp.bfloat16)
    counts = jnp.dot(chosen.astype(jnp.bfloat16), before, preferred_element_type=jnp.float32)
    rank = jnp.sum(jnp.where(chosen, counts, 0.0), axis=0, keepdims=True).astype(jnp.int32) - core * ranks
    mine = (rank >= 0) & (rank < ranks)
    place = jnp.where(mine, source.astype(jnp.int32) * ranks + rank, -1)
    sent = owners * ranks
    select = (iota((sent, entries), 0) == place).astype(jnp.bfloat16)
    blocks = out_ref.shape[0]
    length = sent // blocks
    for i in range(panels_ref.shape[0]):
        part = jnp.dot(select, panels_ref[i], preferred_element_type=jnp.float32).astype(jnp.bfloat16)
        out_ref[:, i * length : (i + 1) * length, :] = part.reshape(blocks, length, LANES)
    group = LANES // ranks
    lane = jnp.where(mine, rank + ranks * (me % group), -1)
    marks = (iota((LANES, entries), 0) == lane).astype(jnp.bfloat16)
    meta = []
    for value in (slot, record):
        table = jnp.where(chosen, value, 0.0).astype(jnp.bfloat16)
        meta.append(lax.dot_general(table, marks, NT, preferred_element_type=jnp.float32).astype(jnp.bfloat16))
    if meta_ref is None:
        tail = jnp.concatenate([m.reshape(owners, 1, LANES) for m in meta] * 4, axis=1)
        out_ref[:, panels_ref.shape[0] * length :, :] = tail
    else:
        for k in range(2):
            meta_ref[k] = meta[k]


META_ROWS = 8


def pack(owners, slots, ranks, tiles, offsets, panels):
    components = panels.shape[0]
    vmem = pl.BlockSpec(memory_space=pltpu.VMEM)
    kernel = functools.partial(pack_kernel, owners, slots, ranks)
    if ranks % 16 == 0:
        return pl.pallas_call(
            kernel,
            out_shape=jax.ShapeDtypeStruct((owners, components * ranks + META_ROWS, LANES), jnp.bfloat16),
            in_specs=[vmem] * 3,
            out_specs=vmem,
            name="pack",
        )(tiles, offsets, panels)
    body, meta = pl.pallas_call(
        kernel,
        out_shape=(
            jax.ShapeDtypeStruct((1, components * owners * ranks, LANES), jnp.bfloat16),
            jax.ShapeDtypeStruct((2, owners, LANES), jnp.bfloat16),
        ),
        in_specs=[vmem] * 3,
        out_specs=(vmem, vmem),
        name="pack",
    )(tiles, offsets, panels)
    body = body.reshape(components, owners, ranks, LANES).transpose(1, 0, 2, 3)
    body = body.reshape(owners, components * ranks, LANES)
    return jnp.concatenate([body, meta.transpose(1, 0, 2)], axis=1)


def unpack(owners, ranks, components, arrived):
    if ranks % 16 == 0:
        return (arrived,)
    body = arrived[:, : components * ranks]
    meta = arrived[:, components * ranks :].transpose(1, 0, 2)
    body = body.reshape(owners, components, ranks, LANES).transpose(1, 0, 2, 3)
    return body.reshape(1, components * owners * ranks, LANES), meta


def planes_for(field, halo):
    return halo if field < 3 or field in (6, 7) else halo - 1


def coded_planes(halo):
    return sum(planes_for(f, halo) + (f < 6) for f in range(FIELDS))


def encode(halo, read, write):
    at = 0
    for field in range(FIELDS):
        near = None
        for k in range(planes_for(field, halo)):
            value = read(field, k)
            if field >= 6:
                parts = [value.astype(jnp.bfloat16)]
            elif near is None:
                high = value.astype(jnp.bfloat16)
                low = (value - high.astype(jnp.float32)).astype(jnp.bfloat16)
                near = high.astype(jnp.float32) + low.astype(jnp.float32)
                parts = [high, low]
            else:
                step = (value - near).astype(jnp.bfloat16)
                near = near + step.astype(jnp.float32)
                parts = [step]
            for part in parts:
                write(at, part)
                at += 1


def decode(halo, read, write):
    at = 0
    for field in range(FIELDS):
        near = None
        for k in range(planes_for(field, halo)):
            value = read(at).astype(jnp.float32)
            at += 1
            if field < 6:
                if near is None:
                    value = value + read(at).astype(jnp.float32)
                    at += 1
                else:
                    value = near + value
                near = value
            write(field, k, value)


def prepare_kernel(halo, *refs):
    disp, prev, lam, mu, buoy = refs[:5]
    outs, fields, sem = refs[5:-2], refs[-2], refs[-1]
    nx, ny, nz = lam.shape
    copies = [
        pltpu.make_async_copy(disp.at[0], fields.at[pl.ds(0, 3)], sem.at[0]),
        pltpu.make_async_copy(prev.at[0], fields.at[pl.ds(3, 3)], sem.at[1]),
        pltpu.make_async_copy(lam, fields.at[6], sem.at[2]),
        pltpu.make_async_copy(mu, fields.at[7], sem.at[3]),
        pltpu.make_async_copy(buoy, fields.at[8], sem.at[4]),
    ]
    for copy in copies:
        copy.start()
    for copy in copies:
        copy.wait()
    odd_x, odd_y = lax.axis_index("gx") % 2, lax.axis_index("gy") % 2

    def coded(p, rows, target):
        def write(at, value):
            target[at] = value

        encode(halo, lambda f, k: fields[f, jnp.where(odd_x == p, nx - 1 - k, k), rows, :], write)

    for p in range(2):
        coded(p, pl.ds(0, ny), outs[p])

    def edge(rows, targets):
        targets[0][...] = fields[:, :, rows, :]
        for p in range(2):
            coded(p, rows, targets[1 + p])

    for q, targets in enumerate((outs[2:5], outs[5:8])):
        if targets:
            pl.when(odd_y == q)(functools.partial(edge, pl.ds(ny - halo, halo), targets))
            pl.when(odd_y != q)(functools.partial(edge, pl.ds(0, halo), targets))


def prepare(halo, ways, disp, prev, lam, mu, buoy):
    nx, ny, nz = lam.shape
    vmem, anywhere = pl.BlockSpec(memory_space=pltpu.VMEM), pl.BlockSpec(memory_space=pl.ANY)
    count = coded_planes(halo)
    edge = [jax.ShapeDtypeStruct((FIELDS, nx, halo, nz), jnp.float32)]
    edge += [jax.ShapeDtypeStruct((count, halo, nz), jnp.bfloat16)] * 2
    shapes = [jax.ShapeDtypeStruct((count, ny, nz), jnp.bfloat16)] * 2 + edge * ways
    return pl.pallas_call(
        functools.partial(prepare_kernel, halo),
        out_shape=shapes,
        in_specs=[anywhere] * 5,
        out_specs=[vmem] * len(shapes),
        scratch_shapes=[pltpu.VMEM((FIELDS, nx, ny, nz), jnp.float32), pltpu.SemaphoreType.DMA((5,))],
        name="prepare",
    )(disp, prev, lam, mu, buoy)


def shifted_up(value, dim):
    return pltpu.roll(value, value.shape[dim] - 1, dim)


def stencil_kernel(halo, *refs):
    disp, prev, lam, mu, buoy = refs[:5]
    halos, (out_ref, strain_ref) = refs[5:-7], refs[-7:-5]
    wave, first, second, scale = refs[-5:-1]
    nx, ny, nz = lam.shape
    tall = ny + 2 * PAD
    odd_x, odd_y = lax.axis_index("gx") % 2, lax.axis_index("gy") % 2
    own_x, own_y = pl.ds(halo, nx), pl.ds(PAD, ny)
    targets = [wave.at[0, i] for i in range(3)] + [wave.at[1, i] for i in range(3)] + [first, second, scale]

    def put(field, xs, ys, value):
        targets[field][xs, ys, :] = value * (TIME_STEP * TIME_STEP) if field == 8 else value

    def spread(p, ys, read):
        def write(field, k, value):
            put(field, jnp.where(odd_x == p, halo + nx + k, halo - 1 - k), ys, value)

        decode(halo, read, write)

    owns = [disp[0, i] for i in range(3)] + [prev[0, i] for i in range(3)] + [lam[...], mu[...], buoy[...]]
    for f, own in enumerate(owns):
        put(f, own_x, own_y, own)
    for p in range(2):
        spread(p, own_y, lambda at, p=p: halos[p][at])
    for upper, ys in ((True, pl.ds(PAD + ny, halo)), (False, pl.ds(PAD - halo, halo))):

        def side(i, at, upper=upper):
            taken = (odd_y == 0) if upper else (odd_y != 0)
            value = halos[2 + i][at].astype(jnp.float32)
            return jnp.where(taken, value, halos[5 + i][at].astype(jnp.float32) if len(halos) > 5 else 0.0)

        for f in range(FIELDS):
            put(f, own_x, ys, side(0, f))
        for p in range(2):
            spread(p, ys, lambda at, p=p, side=side: side(1 + p, at))

    lane = iota((tall, nz), 1)
    not_last, not_first = lane < nz - 1, lane > 0

    def fields(cur, x):
        base = [wave[cur, i, x] for i in range(3)]
        nxt = [wave[cur, i, x + 1] for i in range(3)]
        dx = [n - b for n, b in zip(nxt, base)]
        dy = [shifted_up(b, 0) - b for b in base]
        dz = [jnp.where(not_last, shifted_up(b, 1), 0.0) - b for b in base]
        normal = [dx[0], dy[1], dz[2]]
        twice = [dy[0] + dx[1], dz[0] + dx[2], dz[1] + dy[2]]
        m = second[x]
        volume = first[x] * (normal[0] + normal[1] + normal[2])
        m2 = m + m
        stress = [volume + m2 * e for e in normal] + [m * e for e in twice]
        return base, normal, twice, stress

    def back_y(v):
        return v - pltpu.roll(v, 1, 0)

    def back_z(v):
        return v - jnp.where(not_first, pltpu.roll(v, 1, 1), 0.0)

    def plane(step, cur, own, x, carry):
        base, normal, twice, stress = fields(cur, x)
        if own:
            rows = pl.ds(pl.multiple_of(step * nx * ny + (x - halo) * ny, ny), ny)
            for e, value in enumerate(normal + [0.5 * t for t in twice]):
                strain_ref[rows, e * nz : (e + 1) * nz] = value[PAD : PAD + ny].astype(jnp.bfloat16)
        xx, yy, zz, xy, xz, yz = stress
        forces = [
            (xx - carry[0]) + back_y(xy) + back_z(xz),
            (xy - carry[1]) + back_y(yy) + back_z(yz),
            (xz - carry[2]) + back_y(yz) + back_z(zz),
        ]
        for i in range(3):
            value = 2.0 * base[i] - wave[1 - cur, i, x] + scale[x] * forces[i]
            if step == STEPS - 1:
                out_ref[0, i, x - halo] = value[PAD : PAD + ny]
            else:
                wave[1 - cur, i, x] = value
        return xx, xy, xz

    for step in range(STEPS):
        cur = step % 2
        reach = STEPS - 1 - step
        begin, end = halo - reach, halo + nx + reach
        stress = fields(cur, begin - 1)[3]
        carry = (stress[0], stress[3], stress[4])
        for lo, hi, own in ((begin, halo, False), (halo, halo + nx, True), (halo + nx, end, False)):
            if hi > lo:
                carry = lax.fori_loop(lo, hi, functools.partial(plane, step, cur, own), carry)


def stencil(halo, disp, prev, lam, mu, buoy, halos):
    nx, ny, nz = lam.shape
    tall, wide = ny + 2 * PAD, nx + 2 * halo
    vmem = pl.BlockSpec(memory_space=pltpu.VMEM)
    operands = (disp, prev, lam, mu, buoy, *halos)
    return pl.pallas_call(
        functools.partial(stencil_kernel, halo),
        out_shape=(
            jax.ShapeDtypeStruct((1, 3, nx, ny, nz), jnp.float32),
            jax.ShapeDtypeStruct((STEPS * nx * ny, 6 * nz), jnp.bfloat16),
        ),
        in_specs=[vmem] * len(operands),
        out_specs=(vmem, vmem),
        scratch_shapes=[pltpu.VMEM((2, 3, wide, tall, nz), jnp.float32)]
        + [pltpu.VMEM((wide, tall, nz), jnp.float32)] * 3
        + [pltpu.SMEM((1,), jnp.int32)],
        compiler_params=pltpu.CompilerParams(vmem_limit_bytes=40 << 20),
        cost_estimate=pl.CostEstimate(flops=10**10, transcendentals=10**8, bytes_accessed=10**8),
        name="stencil",
    )(*operands)


def response_kernel(owners, ranks, records, strain_ref, column_ref, *refs):
    points = column_ref.shape[1]
    sent = owners * ranks
    group = LANES // ranks
    columns = strain_ref.shape[0] // STEPS
    total, out_ref = None, refs[-1]
    friendly = ranks % 16 == 0
    for half in range(2):
        pan = refs[half if friendly else 2 * half]
        length = sent // pan.shape[0]
        rows = []
        for k in range(2):
            table = pan[:, 6 * length + k, :] if friendly else refs[2 * half + 1][k]
            table = table.astype(jnp.float32)
            parts = [
                jnp.sum(table[g * group : (g + 1) * group], axis=0, keepdims=True) for g in range(owners // group)
            ]
            rows.append(jnp.concatenate(parts, axis=1))
        slot, record = rows
        owner = iota((1, sent), 1) // ranks
        spread = (iota((points, sent), 0) == slot.astype(jnp.int32)).astype(jnp.bfloat16)
        table = jnp.broadcast_to(column_ref[...].astype(jnp.float32), (8, points)).astype(jnp.bfloat16)
        column = jnp.dot(table, spread, preferred_element_type=jnp.float32)[:1].astype(jnp.int32)
        grid = None
        for i in range(3):
            right = jnp.concatenate(
                [pan[:, (2 * i + k) * length : (2 * i + k + 1) * length, :].reshape(sent, LANES) for k in range(2)],
                axis=1,
            )
            left = strain_ref[:, 2 * i * LANES : (2 * i + 2) * LANES]
            term = lax.dot_general(left, right, NT, preferred_element_type=jnp.float32)
            grid = term if grid is None else grid + term
        mark = iota((columns, sent), 0) == column
        reply = [
            jnp.sum(jnp.where(mark, grid[m * columns : (m + 1) * columns], 0.0), axis=0, keepdims=True)
            for m in range(STEPS)
        ]
        record = record.astype(jnp.int32)
        offset = record % STEPS
        delayed = []
        for n in range(STEPS):
            value = jnp.where(offset == n, reply[0], 0.0)
            for m in range(1, n + 1):
                value = value + jnp.where(offset == n - m, reply[m], 0.0)
            delayed.append(value)
        delayed = jnp.concatenate(delayed + [jnp.zeros((8 - STEPS, sent), jnp.float32)], axis=0)
        key = owner * records + record // STEPS
        gather = (iota((owners * records, sent), 0) == key).astype(jnp.float32)
        part = lax.dot_general(
            delayed, gather, NT, preferred_element_type=jnp.float32, precision=lax.Precision.HIGHEST
        )
        total = part if total is None else total + part
    out_ref[...] = total[:STEPS]


def respond(owners, ranks, records, strain, columns, halves):
    vmem = pl.BlockSpec(memory_space=pltpu.VMEM)
    operands = (strain, columns, *halves[0], *halves[1])
    return pl.pallas_call(
        functools.partial(response_kernel, owners, ranks, records),
        out_shape=jax.ShapeDtypeStruct((STEPS, owners * records), jnp.float32),
        in_specs=[vmem] * len(operands),
        out_specs=vmem,
        compiler_params=pltpu.CompilerParams(vmem_limit_bytes=40 << 20),
        name="respond",
    )(*operands)


def partner(index, length, turn):
    if turn is None:
        return index
    other = index + 1 if index % 2 == turn else index - 1
    return other if 0 <= other < length else None


def exchange(value, gxs, gys, turn_x, turn_y):
    pairs = []
    for i in range(gxs):
        for j in range(gys):
            x, y = partner(i, gxs, turn_x), partner(j, gys, turn_y)
            if x is not None and y is not None:
                pairs.append((i * gys + j, x * gys + y))
    return lax.ppermute(value, OWNERS_AXES, pairs)


def owner_sum(value, owners):
    if owners & (owners - 1):
        return lax.psum(value, OWNERS_AXES)
    bit = 1
    while bit < owners:
        value = value + lax.ppermute(value, OWNERS_AXES, [(i, i ^ bit) for i in range(owners)])
        bit *= 2
    return value


def body(displacement, previous, first_lame, shear_modulus, buoyancy, tile_column, rupture_tiles, slip_offsets, slip_panels):
    gxs, gys = lax.axis_size("gx"), lax.axis_size("gy")
    owners = gxs * gys
    nx, ny, nz = shear_modulus.shape
    halo = STEPS
    slots = tile_column.shape[0]
    records, listed = rupture_tiles.shape
    entries = records * listed
    ranks = entries // owners
    components = slip_panels.shape[2]

    panels = slip_panels.reshape(entries, components, nz).transpose(1, 0, 2)
    payload = pack(owners, slots, ranks, rupture_tiles, slip_offsets, panels)
    arrived = lax.all_to_all(payload, OWNERS_AXES, split_axis=0, concat_axis=0, tiled=True)

    waves = (displacement, previous, first_lame, shear_modulus, buoyancy)
    turns_y = range(1 if gys == 2 else 2)
    gated, _ = lax.optimization_barrier((waves, payload))
    sent = prepare(halo, len(turns_y), *gated)
    ways = [(0, None), (1, None)] + [(x, q) for q in turns_y for x in (None, 0, 1)]
    halos = [exchange(value, gxs, gys, *way) for value, way in zip(sent, ways)]

    arrived, halos = lax.optimization_barrier((arrived, halos))
    other = lax.ppermute(arrived, "comp", [(0, 1), (1, 0)])
    final, strain = stencil(halo, *waves, halos)
    halves = [unpack(owners, ranks, components, v) for v in (arrived, other)]
    partial = respond(owners, ranks, records, strain, tile_column.reshape(1, slots), halves)
    summed = owner_sum(partial, owners)
    mine = lax.dynamic_slice_in_dim(summed, owner_index() * records, records, axis=1)
    return final, mine.T[None]


def solution(mesh):
    in_specs = (
        P("comp", None, ("site", "gx"), "gy", None),
        P("comp", None, ("site", "gx"), "gy", None),
        P(("site", "gx"), "gy", None),
        P(("site", "gx"), "gy", None),
        P(("site", "gx"), "gy", None),
        P(("site", "gx", "gy")),
        P(("site", "gx", "gy"), None),
        P(("site", "gx", "gy"), None),
        P(("site", "gx", "gy"), None, None, None),
    )
    out_specs = (P("comp", None, ("site", "gx"), "gy", None), P("comp", ("site", "gx", "gy"), None))
    return jax.shard_map(body, mesh=mesh, in_specs=in_specs, out_specs=out_specs, check_vma=False)
```

```python
import functools

import jax
import jax.numpy as jnp
from jax import lax
from jax.experimental import pallas as pl
from jax.experimental.pallas import tpu as pltpu
from jax.sharding import PartitionSpec as P

STEPS = 4
TIME_STEP = 0.12
LANES = 128
PAD = 8
OWNERS_AXES = ("gx", "gy")
FIELDS = 9
NT = (((1,), (1,)), ((), ()))


def iota(shape, dim):
    return lax.broadcasted_iota(jnp.int32, shape, dim)


def owner_index():
    return lax.axis_index("gx") * lax.axis_size("gy") + lax.axis_index("gy")


def pack_kernel(owners, slots, ranks, tiles_ref, offsets_ref, panels_ref, out_ref, meta_ref=None):
    rows, cols = tiles_ref.shape
    entries = rows * cols
    core = lax.axis_index("comp")
    me = owner_index()
    tiles = tiles_ref[...]
    shift = slots.bit_length() - 1
    fields = jnp.concatenate([tiles >> shift, tiles & (slots - 1), offsets_ref[...]], axis=0)
    spread = (iota((cols, entries), 1) % cols == iota((cols, entries), 0)).astype(jnp.bfloat16)
    wide = jnp.dot(fields.astype(jnp.float32).astype(jnp.bfloat16), spread, preferred_element_type=jnp.float32)
    lane_row = iota((rows, entries), 1) // cols
    keep = lane_row == iota((rows, entries), 0)
    source, slot, offset = [
        jnp.sum(jnp.where(keep, wide[i * rows : (i + 1) * rows], 0.0), axis=0, keepdims=True) for i in range(3)
    ]
    record = (iota((1, entries), 1) // cols).astype(jnp.float32) * STEPS + offset
    chosen = source == iota((owners, entries), 0).astype(jnp.float32)
    before = (iota((entries, entries), 0) < iota((entries, entries), 1)).astype(jnp.bfloat16)
    counts = jnp.dot(chosen.astype(jnp.bfloat16), before, preferred_element_type=jnp.float32)
    rank = jnp.sum(jnp.where(chosen, counts, 0.0), axis=0, keepdims=True).astype(jnp.int32) - core * ranks
    mine = (rank >= 0) & (rank < ranks)
    place = jnp.where(mine, source.astype(jnp.int32) * ranks + rank, -1)
    sent = owners * ranks
    select = (iota((sent, entries), 0) == place).astype(jnp.bfloat16)
    blocks = out_ref.shape[0]
    length = sent // blocks
    for i in range(panels_ref.shape[0]):
        part = jnp.dot(select, panels_ref[i], preferred_element_type=jnp.float32).astype(jnp.bfloat16)
        out_ref[:, i * length : (i + 1) * length, :] = part.reshape(blocks, length, LANES)
    group = LANES // ranks
    lane = jnp.where(mine, rank + ranks * (me % group), -1)
    marks = (iota((LANES, entries), 0) == lane).astype(jnp.bfloat16)
    meta = []
    for value in (slot, record):
        table = jnp.where(chosen, value, 0.0).astype(jnp.bfloat16)
        meta.append(lax.dot_general(table, marks, NT, preferred_element_type=jnp.float32).astype(jnp.bfloat16))
    if meta_ref is None:
        tail = jnp.concatenate([m.reshape(owners, 1, LANES) for m in meta] * 4, axis=1)
        out_ref[:, panels_ref.shape[0] * length :, :] = tail
    else:
        for k in range(2):
            meta_ref[k] = meta[k]


META_ROWS = 8


def pack(owners, slots, ranks, tiles, offsets, panels):
    components = panels.shape[0]
    vmem = pl.BlockSpec(memory_space=pltpu.VMEM)
    kernel = functools.partial(pack_kernel, owners, slots, ranks)
    if ranks % 16 == 0:
        return pl.pallas_call(
            kernel,
            out_shape=jax.ShapeDtypeStruct((owners, components * ranks + META_ROWS, LANES), jnp.bfloat16),
            in_specs=[vmem] * 3,
            out_specs=vmem,
            name="pack",
        )(tiles, offsets, panels)
    body, meta = pl.pallas_call(
        kernel,
        out_shape=(
            jax.ShapeDtypeStruct((1, components * owners * ranks, LANES), jnp.bfloat16),
            jax.ShapeDtypeStruct((2, owners, LANES), jnp.bfloat16),
        ),
        in_specs=[vmem] * 3,
        out_specs=(vmem, vmem),
        name="pack",
    )(tiles, offsets, panels)
    body = body.reshape(components, owners, ranks, LANES).transpose(1, 0, 2, 3)
    body = body.reshape(owners, components * ranks, LANES)
    return jnp.concatenate([body, meta.transpose(1, 0, 2)], axis=1)


def unpack(owners, ranks, components, arrived):
    if ranks % 16 == 0:
        return (arrived,)
    body = arrived[:, : components * ranks]
    meta = arrived[:, components * ranks :].transpose(1, 0, 2)
    body = body.reshape(owners, components, ranks, LANES).transpose(1, 0, 2, 3)
    return body.reshape(1, components * owners * ranks, LANES), meta


def planes_for(field, halo):
    return halo if field < 3 or field in (6, 7) else halo - 1


def coded_planes(halo):
    return sum(planes_for(f, halo) + (f < 6) for f in range(FIELDS))


def encode(halo, read, write):
    at = 0
    for field in range(FIELDS):
        near = None
        for k in range(planes_for(field, halo)):
            value = read(field, k)
            if field >= 6:
                parts = [value.astype(jnp.bfloat16)]
            elif near is None:
                high = value.astype(jnp.bfloat16)
                low = (value - high.astype(jnp.float32)).astype(jnp.bfloat16)
                near = high.astype(jnp.float32) + low.astype(jnp.float32)
                parts = [high, low]
            else:
                step = (value - near).astype(jnp.bfloat16)
                near = near + step.astype(jnp.float32)
                parts = [step]
            for part in parts:
                write(at, part)
                at += 1


def decode(halo, read, write):
    at = 0
    for field in range(FIELDS):
        near = None
        for k in range(planes_for(field, halo)):
            value = read(at).astype(jnp.float32)
            at += 1
            if field < 6:
                if near is None:
                    value = value + read(at).astype(jnp.float32)
                    at += 1
                else:
                    value = near + value
                near = value
            write(field, k, value)


def prepare_kernel(halo, *refs):
    disp, prev, lam, mu, buoy = refs[:5]
    outs, fields, sem = refs[5:-2], refs[-2], refs[-1]
    nx, ny, nz = lam.shape
    copies = [
        pltpu.make_async_copy(disp.at[0], fields.at[pl.ds(0, 3)], sem.at[0]),
        pltpu.make_async_copy(prev.at[0], fields.at[pl.ds(3, 3)], sem.at[1]),
        pltpu.make_async_copy(lam, fields.at[6], sem.at[2]),
        pltpu.make_async_copy(mu, fields.at[7], sem.at[3]),
        pltpu.make_async_copy(buoy, fields.at[8], sem.at[4]),
    ]
    for copy in copies:
        copy.start()
    for copy in copies:
        copy.wait()
    odd_x, odd_y = lax.axis_index("gx") % 2, lax.axis_index("gy") % 2

    def coded(p, rows, target):
        def write(at, value):
            target[at] = value

        encode(halo, lambda f, k: fields[f, jnp.where(odd_x == p, nx - 1 - k, k), rows, :], write)

    for p in range(2):
        coded(p, pl.ds(0, ny), outs[p])

    def edge(rows, targets):
        targets[0][...] = fields[:, :, rows, :]
        for p in range(2):
            coded(p, rows, targets[1 + p])

    for q, targets in enumerate((outs[2:5], outs[5:8])):
        if targets:
            pl.when(odd_y == q)(functools.partial(edge, pl.ds(ny - halo, halo), targets))
            pl.when(odd_y != q)(functools.partial(edge, pl.ds(0, halo), targets))


def prepare(halo, ways, disp, prev, lam, mu, buoy):
    nx, ny, nz = lam.shape
    vmem, anywhere = pl.BlockSpec(memory_space=pltpu.VMEM), pl.BlockSpec(memory_space=pl.ANY)
    count = coded_planes(halo)
    edge = [jax.ShapeDtypeStruct((FIELDS, nx, halo, nz), jnp.float32)]
    edge += [jax.ShapeDtypeStruct((count, halo, nz), jnp.bfloat16)] * 2
    shapes = [jax.ShapeDtypeStruct((count, ny, nz), jnp.bfloat16)] * 2 + edge * ways
    return pl.pallas_call(
        functools.partial(prepare_kernel, halo),
        out_shape=shapes,
        in_specs=[anywhere] * 5,
        out_specs=[vmem] * len(shapes),
        scratch_shapes=[pltpu.VMEM((FIELDS, nx, ny, nz), jnp.float32), pltpu.SemaphoreType.DMA((5,))],
        name="prepare",
    )(disp, prev, lam, mu, buoy)


def shifted_up(value, dim):
    return pltpu.roll(value, value.shape[dim] - 1, dim)


def stencil_kernel(halo, *refs):
    disp, prev, lam, mu, buoy = refs[:5]
    halos, (out_ref, strain_ref) = refs[5:-7], refs[-7:-5]
    wave, first, second, scale = refs[-5:-1]
    nx, ny, nz = lam.shape
    tall = ny + 2 * PAD
    odd_x, odd_y = lax.axis_index("gx") % 2, lax.axis_index("gy") % 2
    own_x, own_y = pl.ds(halo, nx), pl.ds(PAD, ny)
    targets = [wave.at[0, i] for i in range(3)] + [wave.at[1, i] for i in range(3)] + [first, second, scale]

    def put(field, xs, ys, value):
        targets[field][xs, ys, :] = value * (TIME_STEP * TIME_STEP) if field == 8 else value

    def spread(p, ys, read):
        def write(field, k, value):
            put(field, jnp.where(odd_x == p, halo + nx + k, halo - 1 - k), ys, value)

        decode(halo, read, write)

    owns = [disp[0, i] for i in range(3)] + [prev[0, i] for i in range(3)] + [lam[...], mu[...], buoy[...]]
    for f, own in enumerate(owns):
        put(f, own_x, own_y, own)
    for p in range(2):
        spread(p, own_y, lambda at, p=p: halos[p][at])
    for upper, ys in ((True, pl.ds(PAD + ny, halo)), (False, pl.ds(PAD - halo, halo))):

        def side(i, at, upper=upper):
            taken = (odd_y == 0) if upper else (odd_y != 0)
            value = halos[2 + i][at].astype(jnp.float32)
            return jnp.where(taken, value, halos[5 + i][at].astype(jnp.float32) if len(halos) > 5 else 0.0)

        for f in range(FIELDS):
            put(f, own_x, ys, side(0, f))
        for p in range(2):
            spread(p, ys, lambda at, p=p, side=side: side(1 + p, at))

    lane = iota((tall, nz), 1)
    not_last, not_first = lane < nz - 1, lane > 0

    def fields(cur, x):
        base = [wave[cur, i, x] for i in range(3)]
        nxt = [wave[cur, i, x + 1] for i in range(3)]
        dx = [n - b for n, b in zip(nxt, base)]
        dy = [shifted_up(b, 0) - b for b in base]
        dz = [jnp.where(not_last, shifted_up(b, 1), 0.0) - b for b in base]
        normal = [dx[0], dy[1], dz[2]]
        twice = [dy[0] + dx[1], dz[0] + dx[2], dz[1] + dy[2]]
        m = second[x]
        volume = first[x] * (normal[0] + normal[1] + normal[2])
        m2 = m + m
        stress = [volume + m2 * e for e in normal] + [m * e for e in twice]
        return base, normal, twice, stress

    def back_y(v):
        return v - pltpu.roll(v, 1, 0)

    def back_z(v):
        return v - jnp.where(not_first, pltpu.roll(v, 1, 1), 0.0)

    def plane(step, cur, own, x, carry):
        base, normal, twice, stress = fields(cur, x)
        if own:
            rows = pl.ds(pl.multiple_of(step * nx * ny + (x - halo) * ny, ny), ny)
            for e, value in enumerate(normal + [0.5 * t for t in twice]):
                strain_ref[rows, e * nz : (e + 1) * nz] = value[PAD : PAD + ny].astype(jnp.bfloat16)
        xx, yy, zz, xy, xz, yz = stress
        forces = [
            (xx - carry[0]) + back_y(xy) + back_z(xz),
            (xy - carry[1]) + back_y(yy) + back_z(yz),
            (xz - carry[2]) + back_y(yz) + back_z(zz),
        ]
        for i in range(3):
            value = 2.0 * base[i] - wave[1 - cur, i, x] + scale[x] * forces[i]
            if step == STEPS - 1:
                out_ref[0, i, x - halo] = value[PAD : PAD + ny]
            else:
                wave[1 - cur, i, x] = value
        return xx, xy, xz

    for step in range(STEPS):
        cur = step % 2
        reach = STEPS - 1 - step
        begin, end = halo - reach, halo + nx + reach
        stress = fields(cur, begin - 1)[3]
        carry = (stress[0], stress[3], stress[4])
        for lo, hi, own in ((begin, halo, False), (halo, halo + nx, True), (halo + nx, end, False)):
            if hi > lo:
                carry = lax.fori_loop(lo, hi, functools.partial(plane, step, cur, own), carry)


def stencil(halo, disp, prev, lam, mu, buoy, halos):
    nx, ny, nz = lam.shape
    tall, wide = ny + 2 * PAD, nx + 2 * halo
    vmem = pl.BlockSpec(memory_space=pltpu.VMEM)
    operands = (disp, prev, lam, mu, buoy, *halos)
    return pl.pallas_call(
        functools.partial(stencil_kernel, halo),
        out_shape=(
            jax.ShapeDtypeStruct((1, 3, nx, ny, nz), jnp.float32),
            jax.ShapeDtypeStruct((STEPS * nx * ny, 6 * nz), jnp.bfloat16),
        ),
        in_specs=[vmem] * len(operands),
        out_specs=(vmem, vmem),
        scratch_shapes=[pltpu.VMEM((2, 3, wide, tall, nz), jnp.float32)]
        + [pltpu.VMEM((wide, tall, nz), jnp.float32)] * 3
        + [pltpu.SMEM((1,), jnp.int32)],
        compiler_params=pltpu.CompilerParams(vmem_limit_bytes=40 << 20),
        cost_estimate=pl.CostEstimate(flops=10**10, transcendentals=10**8, bytes_accessed=10**8),
        name="stencil",
    )(*operands)


def response_kernel(owners, ranks, records, strain_ref, column_ref, *refs):
    points = column_ref.shape[1]
    sent = owners * ranks
    group = LANES // ranks
    columns = strain_ref.shape[0] // STEPS
    total, out_ref = None, refs[-1]
    friendly = ranks % 16 == 0
    for half in range(2):
        pan = refs[half if friendly else 2 * half]
        length = sent // pan.shape[0]
        rows = []
        for k in range(2):
            table = pan[:, 6 * length + k, :] if friendly else refs[2 * half + 1][k]
            table = table.astype(jnp.float32)
            parts = [
                jnp.sum(table[g * group : (g + 1) * group], axis=0, keepdims=True) for g in range(owners // group)
            ]
            rows.append(jnp.concatenate(parts, axis=1))
        slot, record = rows
        owner = iota((1, sent), 1) // ranks
        spread = (iota((points, sent), 0) == slot.astype(jnp.int32)).astype(jnp.bfloat16)
        table = jnp.broadcast_to(column_ref[...].astype(jnp.float32), (8, points)).astype(jnp.bfloat16)
        column = jnp.dot(table, spread, preferred_element_type=jnp.float32)[:1].astype(jnp.int32)
        grid = None
        for i in range(3):
            right = jnp.concatenate(
                [pan[:, (2 * i + k) * length : (2 * i + k + 1) * length, :].reshape(sent, LANES) for k in range(2)],
                axis=1,
            )
            left = strain_ref[:, 2 * i * LANES : (2 * i + 2) * LANES]
            term = lax.dot_general(left, right, NT, preferred_element_type=jnp.float32)
            grid = term if grid is None else grid + term
        mark = iota((columns, sent), 0) == column
        reply = [
            jnp.sum(jnp.where(mark, grid[m * columns : (m + 1) * columns], 0.0), axis=0, keepdims=True)
            for m in range(STEPS)
        ]
        record = record.astype(jnp.int32)
        offset = record % STEPS
        delayed = []
        for n in range(STEPS):
            value = jnp.where(offset == n, reply[0], 0.0)
            for m in range(1, n + 1):
                value = value + jnp.where(offset == n - m, reply[m], 0.0)
            delayed.append(value)
        delayed = jnp.concatenate(delayed + [jnp.zeros((8 - STEPS, sent), jnp.float32)], axis=0)
        key = owner * records + record // STEPS
        gather = (iota((owners * records, sent), 0) == key).astype(jnp.float32)
        part = lax.dot_general(
            delayed, gather, NT, preferred_element_type=jnp.float32, precision=lax.Precision.HIGHEST
        )
        total = part if total is None else total + part
    out_ref[...] = total[:STEPS]


def respond(owners, ranks, records, strain, columns, halves):
    vmem = pl.BlockSpec(memory_space=pltpu.VMEM)
    operands = (strain, columns, *halves[0], *halves[1])
    return pl.pallas_call(
        functools.partial(response_kernel, owners, ranks, records),
        out_shape=jax.ShapeDtypeStruct((STEPS, owners * records), jnp.float32),
        in_specs=[vmem] * len(operands),
        out_specs=vmem,
        compiler_params=pltpu.CompilerParams(vmem_limit_bytes=40 << 20),
        name="respond",
    )(*operands)


def partner(index, length, turn):
    if turn is None:
        return index
    other = index + 1 if index % 2 == turn else index - 1
    return other if 0 <= other < length else None


def exchange(value, gxs, gys, turn_x, turn_y):
    pairs = []
    for i in range(gxs):
        for j in range(gys):
            x, y = partner(i, gxs, turn_x), partner(j, gys, turn_y)
            if x is not None and y is not None:
                pairs.append((i * gys + j, x * gys + y))
    return lax.ppermute(value, OWNERS_AXES, pairs)


def owner_sum(value):
    for axis in ("gy", "gx"):
        size = lax.axis_size(axis)
        if size & (size - 1):
            value = lax.psum(value, axis)
        elif size <= 4:
            parts = [lax.ppermute(value, axis, [(i, i ^ k) for i in range(size)]) for k in range(1, size)]
            value = functools.reduce(jnp.add, parts, value)
        else:
            bit = 1
            while bit < size:
                value = value + lax.ppermute(value, axis, [(i, i ^ bit) for i in range(size)])
                bit *= 2
    return value


def body(displacement, previous, first_lame, shear_modulus, buoyancy, tile_column, rupture_tiles, slip_offsets, slip_panels):
    gxs, gys = lax.axis_size("gx"), lax.axis_size("gy")
    owners = gxs * gys
    nx, ny, nz = shear_modulus.shape
    halo = STEPS
    slots = tile_column.shape[0]
    records, listed = rupture_tiles.shape
    entries = records * listed
    ranks = entries // owners
    components = slip_panels.shape[2]

    waves = (displacement, previous, first_lame, shear_modulus, buoyancy)
    turns_y = range(1 if gys == 2 else 2)
    sent = prepare(halo, len(turns_y), *waves)
    ways = [(0, None), (1, None)] + [(x, q) for q in turns_y for x in (None, 0, 1)]
    halos = [exchange(value, gxs, gys, *way) for value, way in zip(sent, ways)]

    halos[2], slip_panels = lax.optimization_barrier((halos[2], slip_panels))
    panels = slip_panels.reshape(entries, components, nz).transpose(1, 0, 2)
    payload = pack(owners, slots, ranks, rupture_tiles, slip_offsets, panels)
    arrived = lax.all_to_all(payload, OWNERS_AXES, split_axis=0, concat_axis=0, tiled=True)

    final, strain = stencil(halo, *waves, halos)
    arrived, strain = lax.optimization_barrier((arrived, strain))
    other = lax.ppermute(arrived, "comp", [(0, 1), (1, 0)])
    halves = [unpack(owners, ranks, components, v) for v in (arrived, other)]
    partial = respond(owners, ranks, records, strain, tile_column.reshape(1, slots), halves)
    summed = owner_sum(partial)
    mine = lax.dynamic_slice_in_dim(summed, owner_index() * records, records, axis=1)
    return final, mine.T[None]


def solution(mesh):
    in_specs = (
        P("comp", None, ("site", "gx"), "gy", None),
        P("comp", None, ("site", "gx"), "gy", None),
        P(("site", "gx"), "gy", None),
        P(("site", "gx"), "gy", None),
        P(("site", "gx"), "gy", None),
        P(("site", "gx", "gy")),
        P(("site", "gx", "gy"), None),
        P(("site", "gx", "gy"), None),
        P(("site", "gx", "gy"), None, None, None),
    )
    out_specs = (P("comp", None, ("site", "gx"), "gy", None), P("comp", ("site", "gx", "gy"), None))
    return jax.shard_map(body, mesh=mesh, in_specs=in_specs, out_specs=out_specs, check_vma=False)
```

```python
import functools

import jax
import jax.numpy as jnp
from jax import lax
from jax.experimental import pallas as pl
from jax.experimental.pallas import tpu as pltpu
from jax.sharding import PartitionSpec as P

STEPS = 4
TIME_STEP = 0.12
LANES = 128
PAD = 8
OWNERS_AXES = ("gx", "gy")
FIELDS = 9
NT = (((1,), (1,)), ((), ()))


def iota(shape, dim):
    return lax.broadcasted_iota(jnp.int32, shape, dim)


def owner_index():
    return lax.axis_index("gx") * lax.axis_size("gy") + lax.axis_index("gy")


def pack_kernel(owners, slots, ranks, tiles_ref, offsets_ref, panels_ref, out_ref, meta_ref=None):
    rows, cols = tiles_ref.shape
    entries = rows * cols
    core = lax.axis_index("comp")
    me = owner_index()
    tiles = tiles_ref[...]
    shift = slots.bit_length() - 1
    fields = jnp.concatenate([tiles >> shift, tiles & (slots - 1), offsets_ref[...]], axis=0)
    spread = (iota((cols, entries), 1) % cols == iota((cols, entries), 0)).astype(jnp.bfloat16)
    wide = jnp.dot(fields.astype(jnp.float32).astype(jnp.bfloat16), spread, preferred_element_type=jnp.float32)
    lane_row = iota((rows, entries), 1) // cols
    keep = lane_row == iota((rows, entries), 0)
    source, slot, offset = [
        jnp.sum(jnp.where(keep, wide[i * rows : (i + 1) * rows], 0.0), axis=0, keepdims=True) for i in range(3)
    ]
    record = (iota((1, entries), 1) // cols).astype(jnp.float32) * STEPS + offset
    chosen = source == iota((owners, entries), 0).astype(jnp.float32)
    before = (iota((entries, entries), 0) < iota((entries, entries), 1)).astype(jnp.bfloat16)
    counts = jnp.dot(chosen.astype(jnp.bfloat16), before, preferred_element_type=jnp.float32)
    rank = jnp.sum(jnp.where(chosen, counts, 0.0), axis=0, keepdims=True).astype(jnp.int32) - core * ranks
    mine = (rank >= 0) & (rank < ranks)
    place = jnp.where(mine, source.astype(jnp.int32) * ranks + rank, -1)
    sent = owners * ranks
    select = (iota((sent, entries), 0) == place).astype(jnp.bfloat16)
    blocks = out_ref.shape[0]
    length = sent // blocks
    for i in range(panels_ref.shape[0]):
        part = jnp.dot(select, panels_ref[i], preferred_element_type=jnp.float32).astype(jnp.bfloat16)
        out_ref[:, i * length : (i + 1) * length, :] = part.reshape(blocks, length, LANES)
    group = LANES // ranks
    lane = jnp.where(mine, rank + ranks * (me % group), -1)
    marks = (iota((LANES, entries), 0) == lane).astype(jnp.bfloat16)
    meta = []
    for value in (slot, record):
        table = jnp.where(chosen, value, 0.0).astype(jnp.bfloat16)
        meta.append(lax.dot_general(table, marks, NT, preferred_element_type=jnp.float32).astype(jnp.bfloat16))
    if meta_ref is None:
        tail = jnp.concatenate([m.reshape(owners, 1, LANES) for m in meta] * 4, axis=1)
        out_ref[:, panels_ref.shape[0] * length :, :] = tail
    else:
        for k in range(2):
            meta_ref[k] = meta[k]


META_ROWS = 8


def pack(owners, slots, ranks, tiles, offsets, panels):
    components = panels.shape[0]
    vmem = pl.BlockSpec(memory_space=pltpu.VMEM)
    kernel = functools.partial(pack_kernel, owners, slots, ranks)
    if ranks % 16 == 0:
        return pl.pallas_call(
            kernel,
            out_shape=jax.ShapeDtypeStruct((owners, components * ranks + META_ROWS, LANES), jnp.bfloat16),
            in_specs=[vmem] * 3,
            out_specs=vmem,
            name="pack",
        )(tiles, offsets, panels)
    body, meta = pl.pallas_call(
        kernel,
        out_shape=(
            jax.ShapeDtypeStruct((1, components * owners * ranks, LANES), jnp.bfloat16),
            jax.ShapeDtypeStruct((2, owners, LANES), jnp.bfloat16),
        ),
        in_specs=[vmem] * 3,
        out_specs=(vmem, vmem),
        name="pack",
    )(tiles, offsets, panels)
    body = body.reshape(components, owners, ranks, LANES).transpose(1, 0, 2, 3)
    body = body.reshape(owners, components * ranks, LANES)
    return jnp.concatenate([body, meta.transpose(1, 0, 2)], axis=1)


def unpack(owners, ranks, components, arrived):
    if ranks % 16 == 0:
        return (arrived,)
    body = arrived[:, : components * ranks]
    meta = arrived[:, components * ranks :].transpose(1, 0, 2)
    body = body.reshape(owners, components, ranks, LANES).transpose(1, 0, 2, 3)
    return body.reshape(1, components * owners * ranks, LANES), meta


def planes_for(field, halo):
    return halo if field < 3 or field in (6, 7) else halo - 1


def coded_planes(halo):
    return sum(planes_for(f, halo) + (f < 6) for f in range(FIELDS))


def encode(halo, read, write):
    at = 0
    for field in range(FIELDS):
        near = None
        for k in range(planes_for(field, halo)):
            value = read(field, k)
            if field >= 6:
                parts = [value.astype(jnp.bfloat16)]
            elif near is None:
                high = value.astype(jnp.bfloat16)
                low = (value - high.astype(jnp.float32)).astype(jnp.bfloat16)
                near = high.astype(jnp.float32) + low.astype(jnp.float32)
                parts = [high, low]
            else:
                step = (value - near).astype(jnp.bfloat16)
                near = near + step.astype(jnp.float32)
                parts = [step]
            for part in parts:
                write(at, part)
                at += 1


def decode(halo, read, write):
    at = 0
    for field in range(FIELDS):
        near = None
        for k in range(planes_for(field, halo)):
            value = read(at).astype(jnp.float32)
            at += 1
            if field < 6:
                if near is None:
                    value = value + read(at).astype(jnp.float32)
                    at += 1
                else:
                    value = near + value
                near = value
            write(field, k, value)


def prepare_kernel(halo, *refs):
    disp, prev, lam, mu, buoy = refs[:5]
    outs, fields, sem = refs[5:-2], refs[-2], refs[-1]
    nx, ny, nz = lam.shape
    copies = [
        pltpu.make_async_copy(disp.at[0], fields.at[pl.ds(0, 3)], sem.at[0]),
        pltpu.make_async_copy(prev.at[0], fields.at[pl.ds(3, 3)], sem.at[1]),
        pltpu.make_async_copy(lam, fields.at[6], sem.at[2]),
        pltpu.make_async_copy(mu, fields.at[7], sem.at[3]),
        pltpu.make_async_copy(buoy, fields.at[8], sem.at[4]),
    ]
    for copy in copies:
        copy.start()
    for copy in copies:
        copy.wait()
    odd_x, odd_y = lax.axis_index("gx") % 2, lax.axis_index("gy") % 2

    def coded(p, rows, target):
        def write(at, value):
            target[at] = value

        encode(halo, lambda f, k: fields[f, jnp.where(odd_x == p, nx - 1 - k, k), rows, :], write)

    for p in range(2):
        coded(p, pl.ds(0, ny), outs[p])

    def edge(rows, targets):
        targets[0][...] = fields[:, :, rows, :]
        for p in range(2):
            coded(p, rows, targets[1 + p])

    for q, targets in enumerate((outs[2:5], outs[5:8])):
        if targets:
            pl.when(odd_y == q)(functools.partial(edge, pl.ds(ny - halo, halo), targets))
            pl.when(odd_y != q)(functools.partial(edge, pl.ds(0, halo), targets))


def prepare(halo, ways, disp, prev, lam, mu, buoy):
    nx, ny, nz = lam.shape
    vmem, anywhere = pl.BlockSpec(memory_space=pltpu.VMEM), pl.BlockSpec(memory_space=pl.ANY)
    count = coded_planes(halo)
    edge = [jax.ShapeDtypeStruct((FIELDS, nx, halo, nz), jnp.float32)]
    edge += [jax.ShapeDtypeStruct((count, halo, nz), jnp.bfloat16)] * 2
    shapes = [jax.ShapeDtypeStruct((count, ny, nz), jnp.bfloat16)] * 2 + edge * ways
    return pl.pallas_call(
        functools.partial(prepare_kernel, halo),
        out_shape=shapes,
        in_specs=[anywhere] * 5,
        out_specs=[vmem] * len(shapes),
        scratch_shapes=[pltpu.VMEM((FIELDS, nx, ny, nz), jnp.float32), pltpu.SemaphoreType.DMA((5,))],
        name="prepare",
    )(disp, prev, lam, mu, buoy)


def shifted_up(value, dim):
    return pltpu.roll(value, value.shape[dim] - 1, dim)


def stencil_kernel(halo, *refs):
    disp, prev, lam, mu, buoy = refs[:5]
    halos, (out_ref, strain_ref) = refs[5:-7], refs[-7:-5]
    wave, first, second, scale = refs[-5:-1]
    nx, ny, nz = lam.shape
    tall = ny + 2 * PAD
    odd_x, odd_y = lax.axis_index("gx") % 2, lax.axis_index("gy") % 2
    own_x, own_y = pl.ds(halo, nx), pl.ds(PAD, ny)
    targets = [wave.at[0, i] for i in range(3)] + [wave.at[1, i] for i in range(3)] + [first, second, scale]

    def put(field, xs, ys, value):
        targets[field][xs, ys, :] = value * (TIME_STEP * TIME_STEP) if field == 8 else value

    def spread(p, ys, read):
        def write(field, k, value):
            put(field, jnp.where(odd_x == p, halo + nx + k, halo - 1 - k), ys, value)

        decode(halo, read, write)

    owns = [disp[0, i] for i in range(3)] + [prev[0, i] for i in range(3)] + [lam[...], mu[...], buoy[...]]
    for f, own in enumerate(owns):
        put(f, own_x, own_y, own)
    for p in range(2):
        spread(p, own_y, lambda at, p=p: halos[p][at])
    for upper, ys in ((True, pl.ds(PAD + ny, halo)), (False, pl.ds(PAD - halo, halo))):

        def side(i, at, upper=upper):
            taken = (odd_y == 0) if upper else (odd_y != 0)
            value = halos[2 + i][at].astype(jnp.float32)
            return jnp.where(taken, value, halos[5 + i][at].astype(jnp.float32) if len(halos) > 5 else 0.0)

        for f in range(FIELDS):
            put(f, own_x, ys, side(0, f))
        for p in range(2):
            spread(p, ys, lambda at, p=p, side=side: side(1 + p, at))

    lane = iota((tall, nz), 1)
    not_last, not_first = lane < nz - 1, lane > 0

    def fields(cur, x):
        base = [wave[cur, i, x] for i in range(3)]
        nxt = [wave[cur, i, x + 1] for i in range(3)]
        dx = [n - b for n, b in zip(nxt, base)]
        dy = [shifted_up(b, 0) - b for b in base]
        dz = [jnp.where(not_last, shifted_up(b, 1), 0.0) - b for b in base]
        normal = [dx[0], dy[1], dz[2]]
        twice = [dy[0] + dx[1], dz[0] + dx[2], dz[1] + dy[2]]
        m = second[x]
        volume = first[x] * (normal[0] + normal[1] + normal[2])
        m2 = m + m
        stress = [volume + m2 * e for e in normal] + [m * e for e in twice]
        return base, normal, twice, stress

    def back_y(v):
        return v - pltpu.roll(v, 1, 0)

    def back_z(v):
        return v - jnp.where(not_first, pltpu.roll(v, 1, 1), 0.0)

    def plane(step, cur, own, x, carry):
        base, normal, twice, stress = fields(cur, x)
        if own:
            rows = pl.ds(pl.multiple_of(step * nx * ny + (x - halo) * ny, ny), ny)
            for e, value in enumerate(normal + [0.5 * t for t in twice]):
                strain_ref[rows, e * nz : (e + 1) * nz] = value[PAD : PAD + ny].astype(jnp.bfloat16)
        xx, yy, zz, xy, xz, yz = stress
        forces = [
            (xx - carry[0]) + back_y(xy) + back_z(xz),
            (xy - carry[1]) + back_y(yy) + back_z(yz),
            (xz - carry[2]) + back_y(yz) + back_z(zz),
        ]
        for i in range(3):
            value = 2.0 * base[i] - wave[1 - cur, i, x] + scale[x] * forces[i]
            if step == STEPS - 1:
                out_ref[0, i, x - halo] = value[PAD : PAD + ny]
            else:
                wave[1 - cur, i, x] = value
        return xx, xy, xz

    for step in range(STEPS):
        cur = step % 2
        reach = STEPS - 1 - step
        begin, end = halo - reach, halo + nx + reach
        stress = fields(cur, begin - 1)[3]
        carry = (stress[0], stress[3], stress[4])
        for lo, hi, own in ((begin, halo, False), (halo, halo + nx, True), (halo + nx, end, False)):
            if hi > lo:
                carry = lax.fori_loop(lo, hi, functools.partial(plane, step, cur, own), carry)


def stencil(halo, disp, prev, lam, mu, buoy, halos):
    nx, ny, nz = lam.shape
    tall, wide = ny + 2 * PAD, nx + 2 * halo
    vmem = pl.BlockSpec(memory_space=pltpu.VMEM)
    operands = (disp, prev, lam, mu, buoy, *halos)
    return pl.pallas_call(
        functools.partial(stencil_kernel, halo),
        out_shape=(
            jax.ShapeDtypeStruct((1, 3, nx, ny, nz), jnp.float32),
            jax.ShapeDtypeStruct((STEPS * nx * ny, 6 * nz), jnp.bfloat16),
        ),
        in_specs=[vmem] * len(operands),
        out_specs=(vmem, vmem),
        scratch_shapes=[pltpu.VMEM((2, 3, wide, tall, nz), jnp.float32)]
        + [pltpu.VMEM((wide, tall, nz), jnp.float32)] * 3
        + [pltpu.SMEM((1,), jnp.int32)],
        compiler_params=pltpu.CompilerParams(vmem_limit_bytes=40 << 20),
        cost_estimate=pl.CostEstimate(flops=10**10, transcendentals=10**8, bytes_accessed=10**8),
        name="stencil",
    )(*operands)


def response_kernel(owners, ranks, records, strain_ref, column_ref, *refs):
    points = column_ref.shape[1]
    sent = owners * ranks
    group = LANES // ranks
    columns = strain_ref.shape[0] // STEPS
    total, out_ref = None, refs[-1]
    friendly = ranks % 16 == 0
    for half in range(2):
        pan = refs[half if friendly else 2 * half]
        length = sent // pan.shape[0]
        rows = []
        for k in range(2):
            table = pan[:, 6 * length + k, :] if friendly else refs[2 * half + 1][k]
            table = table.astype(jnp.float32)
            parts = [
                jnp.sum(table[g * group : (g + 1) * group], axis=0, keepdims=True) for g in range(owners // group)
            ]
            rows.append(jnp.concatenate(parts, axis=1))
        slot, record = rows
        owner = iota((1, sent), 1) // ranks
        spread = (iota((points, sent), 0) == slot.astype(jnp.int32)).astype(jnp.bfloat16)
        table = jnp.broadcast_to(column_ref[...].astype(jnp.float32), (8, points)).astype(jnp.bfloat16)
        column = jnp.dot(table, spread, preferred_element_type=jnp.float32)[:1].astype(jnp.int32)
        grid = None
        for i in range(3):
            right = jnp.concatenate(
                [pan[:, (2 * i + k) * length : (2 * i + k + 1) * length, :].reshape(sent, LANES) for k in range(2)],
                axis=1,
            )
            left = strain_ref[:, 2 * i * LANES : (2 * i + 2) * LANES]
            term = lax.dot_general(left, right, NT, preferred_element_type=jnp.float32)
            grid = term if grid is None else grid + term
        mark = iota((columns, sent), 0) == column
        reply = [
            jnp.sum(jnp.where(mark, grid[m * columns : (m + 1) * columns], 0.0), axis=0, keepdims=True)
            for m in range(STEPS)
        ]
        record = record.astype(jnp.int32)
        offset = record % STEPS
        delayed = []
        for n in range(STEPS):
            value = jnp.where(offset == n, reply[0], 0.0)
            for m in range(1, n + 1):
                value = value + jnp.where(offset == n - m, reply[m], 0.0)
            delayed.append(value)
        delayed = jnp.concatenate(delayed + [jnp.zeros((8 - STEPS, sent), jnp.float32)], axis=0)
        key = owner * records + record // STEPS
        gather = (iota((owners * records, sent), 0) == key).astype(jnp.float32)
        part = lax.dot_general(
            delayed, gather, NT, preferred_element_type=jnp.float32, precision=lax.Precision.HIGHEST
        )
        total = part if total is None else total + part
    for s in range(owners):
        out_ref[s] = total[:STEPS, s * records : (s + 1) * records]


def respond(owners, ranks, records, strain, columns, halves):
    vmem = pl.BlockSpec(memory_space=pltpu.VMEM)
    operands = (strain, columns, *halves[0], *halves[1])
    return pl.pallas_call(
        functools.partial(response_kernel, owners, ranks, records),
        out_shape=jax.ShapeDtypeStruct((owners, STEPS, records), jnp.float32),
        in_specs=[vmem] * len(operands),
        out_specs=vmem,
        compiler_params=pltpu.CompilerParams(vmem_limit_bytes=40 << 20),
        name="respond",
    )(*operands)


def partner(index, length, turn):
    if turn is None:
        return index
    other = index + 1 if index % 2 == turn else index - 1
    return other if 0 <= other < length else None


def exchange(value, gxs, gys, turn_x, turn_y):
    pairs = []
    for i in range(gxs):
        for j in range(gys):
            x, y = partner(i, gxs, turn_x), partner(j, gys, turn_y)
            if x is not None and y is not None:
                pairs.append((i * gys + j, x * gys + y))
    return lax.ppermute(value, OWNERS_AXES, pairs)


def body(displacement, previous, first_lame, shear_modulus, buoyancy, tile_column, rupture_tiles, slip_offsets, slip_panels):
    gxs, gys = lax.axis_size("gx"), lax.axis_size("gy")
    owners = gxs * gys
    nx, ny, nz = shear_modulus.shape
    halo = STEPS
    slots = tile_column.shape[0]
    records, listed = rupture_tiles.shape
    entries = records * listed
    ranks = entries // owners
    components = slip_panels.shape[2]

    waves = (displacement, previous, first_lame, shear_modulus, buoyancy)
    turns_y = range(1 if gys == 2 else 2)
    sent = prepare(halo, len(turns_y), *waves)
    ways = [(0, None), (1, None)] + [(x, q) for q in turns_y for x in (None, 0, 1)]
    slip_panels, sent = lax.optimization_barrier((slip_panels, sent))
    halos = [exchange(value, gxs, gys, *way) for value, way in zip(sent, ways)]

    panels = slip_panels.reshape(entries, components, nz).transpose(1, 0, 2)
    payload = pack(owners, slots, ranks, rupture_tiles, slip_offsets, panels)
    arrived = lax.all_to_all(payload, OWNERS_AXES, split_axis=0, concat_axis=0, tiled=True)

    final, strain = stencil(halo, *waves, halos)
    arrived, strain = lax.optimization_barrier((arrived, strain))
    other = lax.ppermute(arrived, "comp", [(0, 1), (1, 0)])
    halves = [unpack(owners, ranks, components, v) for v in (arrived, other)]
    partial = respond(owners, ranks, records, strain, tile_column.reshape(1, slots), halves)
    shares = lax.all_to_all(partial, OWNERS_AXES, split_axis=0, concat_axis=0, tiled=True)
    return final, jnp.sum(shares, axis=0).T[None]


def solution(mesh):
    in_specs = (
        P("comp", None, ("site", "gx"), "gy", None),
        P("comp", None, ("site", "gx"), "gy", None),
        P(("site", "gx"), "gy", None),
        P(("site", "gx"), "gy", None),
        P(("site", "gx"), "gy", None),
        P(("site", "gx", "gy")),
        P(("site", "gx", "gy"), None),
        P(("site", "gx", "gy"), None),
        P(("site", "gx", "gy"), None, None, None),
    )
    out_specs = (P("comp", None, ("site", "gx"), "gy", None), P("comp", ("site", "gx", "gy"), None))
    return jax.shard_map(body, mesh=mesh, in_specs=in_specs, out_specs=out_specs, check_vma=False)
```

```python
import functools

import jax
import jax.numpy as jnp
from jax import lax
from jax.experimental import pallas as pl
from jax.experimental.pallas import tpu as pltpu
from jax.sharding import PartitionSpec as P

STEPS = 4
TIME_STEP = 0.12
LANES = 128
PAD = 8
OWNERS_AXES = ("gx", "gy")
FIELDS = 9
NT = (((1,), (1,)), ((), ()))


def iota(shape, dim):
    return lax.broadcasted_iota(jnp.int32, shape, dim)


def owner_index():
    return lax.axis_index("gx") * lax.axis_size("gy") + lax.axis_index("gy")


def pack_kernel(owners, slots, ranks, tiles_ref, offsets_ref, panels_ref, out_ref, meta_ref=None):
    rows, cols = tiles_ref.shape
    entries = rows * cols
    core = lax.axis_index("comp")
    me = owner_index()
    tiles = tiles_ref[...]
    shift = slots.bit_length() - 1
    fields = jnp.concatenate([tiles >> shift, tiles & (slots - 1), offsets_ref[...]], axis=0)
    spread = (iota((cols, entries), 1) % cols == iota((cols, entries), 0)).astype(jnp.bfloat16)
    wide = jnp.dot(fields.astype(jnp.float32).astype(jnp.bfloat16), spread, preferred_element_type=jnp.float32)
    lane_row = iota((rows, entries), 1) // cols
    keep = lane_row == iota((rows, entries), 0)
    source, slot, offset = [
        jnp.sum(jnp.where(keep, wide[i * rows : (i + 1) * rows], 0.0), axis=0, keepdims=True) for i in range(3)
    ]
    record = (iota((1, entries), 1) // cols).astype(jnp.float32) * STEPS + offset
    chosen = source == iota((owners, entries), 0).astype(jnp.float32)
    before = (iota((entries, entries), 0) < iota((entries, entries), 1)).astype(jnp.bfloat16)
    counts = jnp.dot(chosen.astype(jnp.bfloat16), before, preferred_element_type=jnp.float32)
    rank = jnp.sum(jnp.where(chosen, counts, 0.0), axis=0, keepdims=True).astype(jnp.int32) - core * ranks
    mine = (rank >= 0) & (rank < ranks)
    place = jnp.where(mine, source.astype(jnp.int32) * ranks + rank, -1)
    sent = owners * ranks
    select = (iota((sent, entries), 0) == place).astype(jnp.bfloat16)
    blocks = out_ref.shape[0]
    length = sent // blocks
    components = panels_ref.shape[1]
    for i in range(components):
        part = jnp.dot(select, panels_ref[:, i].reshape(entries, LANES), preferred_element_type=jnp.float32).astype(jnp.bfloat16)
        out_ref[:, i * length : (i + 1) * length, :] = part.reshape(blocks, length, LANES)
    group = LANES // ranks
    lane = jnp.where(mine, rank + ranks * (me % group), -1)
    marks = (iota((LANES, entries), 0) == lane).astype(jnp.bfloat16)
    meta = []
    for value in (slot, record):
        table = jnp.where(chosen, value, 0.0).astype(jnp.bfloat16)
        meta.append(lax.dot_general(table, marks, NT, preferred_element_type=jnp.float32).astype(jnp.bfloat16))
    if meta_ref is None:
        tail = jnp.concatenate([m.reshape(owners, 1, LANES) for m in meta] * 4, axis=1)
        out_ref[:, components * length :, :] = tail
    else:
        for k in range(2):
            meta_ref[k] = meta[k]


META_ROWS = 8


def pack(owners, slots, ranks, tiles, offsets, panels):
    components = panels.shape[1]
    vmem = pl.BlockSpec(memory_space=pltpu.VMEM)
    kernel = functools.partial(pack_kernel, owners, slots, ranks)
    if ranks % 16 == 0:
        return pl.pallas_call(
            kernel,
            out_shape=jax.ShapeDtypeStruct((owners, components * ranks + META_ROWS, LANES), jnp.bfloat16),
            in_specs=[vmem] * 3,
            out_specs=vmem,
            name="pack",
        )(tiles, offsets, panels)
    body, meta = pl.pallas_call(
        kernel,
        out_shape=(
            jax.ShapeDtypeStruct((1, components * owners * ranks, LANES), jnp.bfloat16),
            jax.ShapeDtypeStruct((2, owners, LANES), jnp.bfloat16),
        ),
        in_specs=[vmem] * 3,
        out_specs=(vmem, vmem),
        name="pack",
    )(tiles, offsets, panels)
    body = body.reshape(components, owners, ranks, LANES).transpose(1, 0, 2, 3)
    body = body.reshape(owners, components * ranks, LANES)
    return jnp.concatenate([body, meta.transpose(1, 0, 2)], axis=1)


def unpack(owners, ranks, components, arrived):
    if ranks % 16 == 0:
        return (arrived,)
    body = arrived[:, : components * ranks]
    meta = arrived[:, components * ranks :].transpose(1, 0, 2)
    body = body.reshape(owners, components, ranks, LANES).transpose(1, 0, 2, 3)
    return body.reshape(1, components * owners * ranks, LANES), meta


def planes_for(field, halo):
    return halo if field < 3 or field in (6, 7) else halo - 1


def coded_planes(halo):
    return sum(planes_for(f, halo) + (f < 6) for f in range(FIELDS))


def encode(halo, read, write):
    at = 0
    for field in range(FIELDS):
        near = None
        for k in range(planes_for(field, halo)):
            value = read(field, k)
            if field >= 6:
                parts = [value.astype(jnp.bfloat16)]
            elif near is None:
                high = value.astype(jnp.bfloat16)
                low = (value - high.astype(jnp.float32)).astype(jnp.bfloat16)
                near = high.astype(jnp.float32) + low.astype(jnp.float32)
                parts = [high, low]
            else:
                step = (value - near).astype(jnp.bfloat16)
                near = near + step.astype(jnp.float32)
                parts = [step]
            for part in parts:
                write(at, part)
                at += 1


def decode(halo, read, write):
    at = 0
    for field in range(FIELDS):
        near = None
        for k in range(planes_for(field, halo)):
            value = read(at).astype(jnp.float32)
            at += 1
            if field < 6:
                if near is None:
                    value = value + read(at).astype(jnp.float32)
                    at += 1
                else:
                    value = near + value
                near = value
            write(field, k, value)


def prepare_kernel(halo, *refs):
    disp, prev, lam, mu, buoy = refs[:5]
    outs, fields, sem = refs[5:-2], refs[-2], refs[-1]
    nx, ny, nz = lam.shape
    copies = [
        pltpu.make_async_copy(disp.at[0], fields.at[pl.ds(0, 3)], sem.at[0]),
        pltpu.make_async_copy(prev.at[0], fields.at[pl.ds(3, 3)], sem.at[1]),
        pltpu.make_async_copy(lam, fields.at[6], sem.at[2]),
        pltpu.make_async_copy(mu, fields.at[7], sem.at[3]),
        pltpu.make_async_copy(buoy, fields.at[8], sem.at[4]),
    ]
    for copy in copies:
        copy.start()
    for copy in copies:
        copy.wait()
    odd_x, odd_y = lax.axis_index("gx") % 2, lax.axis_index("gy") % 2

    def coded(p, rows, target):
        def write(at, value):
            target[at] = value

        encode(halo, lambda f, k: fields[f, jnp.where(odd_x == p, nx - 1 - k, k), rows, :], write)

    for p in range(2):
        coded(p, pl.ds(0, ny), outs[p])

    def edge(rows, targets):
        targets[0][...] = fields[:, :, rows, :]
        for p in range(2):
            coded(p, rows, targets[1 + p])

    for q, targets in enumerate((outs[2:5], outs[5:8])):
        if targets:
            pl.when(odd_y == q)(functools.partial(edge, pl.ds(ny - halo, halo), targets))
            pl.when(odd_y != q)(functools.partial(edge, pl.ds(0, halo), targets))


def prepare(halo, ways, disp, prev, lam, mu, buoy):
    nx, ny, nz = lam.shape
    vmem, anywhere = pl.BlockSpec(memory_space=pltpu.VMEM), pl.BlockSpec(memory_space=pl.ANY)
    count = coded_planes(halo)
    edge = [jax.ShapeDtypeStruct((FIELDS, nx, halo, nz), jnp.float32)]
    edge += [jax.ShapeDtypeStruct((count, halo, nz), jnp.bfloat16)] * 2
    shapes = [jax.ShapeDtypeStruct((count, ny, nz), jnp.bfloat16)] * 2 + edge * ways
    return pl.pallas_call(
        functools.partial(prepare_kernel, halo),
        out_shape=shapes,
        in_specs=[anywhere] * 5,
        out_specs=[vmem] * len(shapes),
        scratch_shapes=[pltpu.VMEM((FIELDS, nx, ny, nz), jnp.float32), pltpu.SemaphoreType.DMA((5,))],
        name="prepare",
    )(disp, prev, lam, mu, buoy)


def shifted_up(value, dim):
    return pltpu.roll(value, value.shape[dim] - 1, dim)


def stencil_kernel(halo, *refs):
    disp, prev, lam, mu, buoy = refs[:5]
    halos, (out_ref, strain_ref) = refs[5:-7], refs[-7:-5]
    wave, first, second, scale = refs[-5:-1]
    nx, ny, nz = lam.shape
    tall = ny + 2 * PAD
    odd_x, odd_y = lax.axis_index("gx") % 2, lax.axis_index("gy") % 2
    own_x, own_y = pl.ds(halo, nx), pl.ds(PAD, ny)
    targets = [wave.at[0, i] for i in range(3)] + [wave.at[1, i] for i in range(3)] + [first, second, scale]

    def put(field, xs, ys, value):
        targets[field][xs, ys, :] = value * (TIME_STEP * TIME_STEP) if field == 8 else value

    def spread(p, ys, read):
        def write(field, k, value):
            put(field, jnp.where(odd_x == p, halo + nx + k, halo - 1 - k), ys, value)

        decode(halo, read, write)

    owns = [disp[0, i] for i in range(3)] + [prev[0, i] for i in range(3)] + [lam[...], mu[...], buoy[...]]
    for f, own in enumerate(owns):
        put(f, own_x, own_y, own)
    for p in range(2):
        spread(p, own_y, lambda at, p=p: halos[p][at])
    for upper, ys in ((True, pl.ds(PAD + ny, halo)), (False, pl.ds(PAD - halo, halo))):

        def side(i, at, upper=upper):
            taken = (odd_y == 0) if upper else (odd_y != 0)
            value = halos[2 + i][at].astype(jnp.float32)
            return jnp.where(taken, value, halos[5 + i][at].astype(jnp.float32) if len(halos) > 5 else 0.0)

        for f in range(FIELDS):
            put(f, own_x, ys, side(0, f))
        for p in range(2):
            spread(p, ys, lambda at, p=p, side=side: side(1 + p, at))

    lane = iota((tall, nz), 1)
    not_last, not_first = lane < nz - 1, lane > 0

    def fields(cur, x):
        base = [wave[cur, i, x] for i in range(3)]
        nxt = [wave[cur, i, x + 1] for i in range(3)]
        dx = [n - b for n, b in zip(nxt, base)]
        dy = [shifted_up(b, 0) - b for b in base]
        dz = [jnp.where(not_last, shifted_up(b, 1), 0.0) - b for b in base]
        normal = [dx[0], dy[1], dz[2]]
        twice = [dy[0] + dx[1], dz[0] + dx[2], dz[1] + dy[2]]
        m = second[x]
        volume = first[x] * (normal[0] + normal[1] + normal[2])
        m2 = m + m
        stress = [volume + m2 * e for e in normal] + [m * e for e in twice]
        return base, normal, twice, stress

    def back_y(v):
        return v - pltpu.roll(v, 1, 0)

    def back_z(v):
        return v - jnp.where(not_first, pltpu.roll(v, 1, 1), 0.0)

    def plane(step, cur, own, x, carry):
        base, normal, twice, stress = fields(cur, x)
        if own:
            rows = pl.ds(pl.multiple_of(step * nx * ny + (x - halo) * ny, ny), ny)
            for e, value in enumerate(normal + [0.5 * t for t in twice]):
                strain_ref[rows, e * nz : (e + 1) * nz] = value[PAD : PAD + ny].astype(jnp.bfloat16)
        xx, yy, zz, xy, xz, yz = stress
        forces = [
            (xx - carry[0]) + back_y(xy) + back_z(xz),
            (xy - carry[1]) + back_y(yy) + back_z(yz),
            (xz - carry[2]) + back_y(yz) + back_z(zz),
        ]
        for i in range(3):
            value = 2.0 * base[i] - wave[1 - cur, i, x] + scale[x] * forces[i]
            if step == STEPS - 1:
                out_ref[0, i, x - halo] = value[PAD : PAD + ny]
            else:
                wave[1 - cur, i, x] = value
        return xx, xy, xz

    for step in range(STEPS):
        cur = step % 2
        reach = STEPS - 1 - step
        begin, end = halo - reach, halo + nx + reach
        stress = fields(cur, begin - 1)[3]
        carry = (stress[0], stress[3], stress[4])
        for lo, hi, own in ((begin, halo, False), (halo, halo + nx, True), (halo + nx, end, False)):
            if hi > lo:
                carry = lax.fori_loop(lo, hi, functools.partial(plane, step, cur, own), carry)


def stencil(halo, disp, prev, lam, mu, buoy, halos):
    nx, ny, nz = lam.shape
    tall, wide = ny + 2 * PAD, nx + 2 * halo
    vmem = pl.BlockSpec(memory_space=pltpu.VMEM)
    operands = (disp, prev, lam, mu, buoy, *halos)
    return pl.pallas_call(
        functools.partial(stencil_kernel, halo),
        out_shape=(
            jax.ShapeDtypeStruct((1, 3, nx, ny, nz), jnp.float32),
            jax.ShapeDtypeStruct((STEPS * nx * ny, 6 * nz), jnp.bfloat16),
        ),
        in_specs=[vmem] * len(operands),
        out_specs=(vmem, vmem),
        scratch_shapes=[pltpu.VMEM((2, 3, wide, tall, nz), jnp.float32)]
        + [pltpu.VMEM((wide, tall, nz), jnp.float32)] * 3
        + [pltpu.SMEM((1,), jnp.int32)],
        compiler_params=pltpu.CompilerParams(vmem_limit_bytes=40 << 20),
        cost_estimate=pl.CostEstimate(flops=10**10, transcendentals=10**8, bytes_accessed=10**8),
        name="stencil",
    )(*operands)


def response_kernel(owners, ranks, records, strain_ref, column_ref, *refs):
    points = column_ref.shape[1]
    sent = owners * ranks
    group = LANES // ranks
    columns = strain_ref.shape[0] // STEPS
    pan, out_ref = refs[0], refs[-1]
    friendly = ranks % 16 == 0
    earlier = refs[-2] if len(refs) > (2 if friendly else 3) else None
    length = sent // pan.shape[0]
    rows = []
    for k in range(2):
        table = pan[:, 6 * length + k, :] if friendly else refs[1][k]
        table = table.astype(jnp.float32)
        parts = [
            jnp.sum(table[g * group : (g + 1) * group], axis=0, keepdims=True) for g in range(owners // group)
        ]
        rows.append(jnp.concatenate(parts, axis=1))
    slot, record = rows
    owner = iota((1, sent), 1) // ranks
    spread = (iota((points, sent), 0) == slot.astype(jnp.int32)).astype(jnp.bfloat16)
    table = jnp.broadcast_to(column_ref[...].astype(jnp.float32), (8, points)).astype(jnp.bfloat16)
    column = jnp.dot(table, spread, preferred_element_type=jnp.float32)[:1].astype(jnp.int32)
    grid = None
    for i in range(3):
        right = jnp.concatenate(
            [pan[:, (2 * i + k) * length : (2 * i + k + 1) * length, :].reshape(sent, LANES) for k in range(2)],
            axis=1,
        )
        left = strain_ref[:, 2 * i * LANES : (2 * i + 2) * LANES]
        term = lax.dot_general(left, right, NT, preferred_element_type=jnp.float32)
        grid = term if grid is None else grid + term
    mark = iota((columns, sent), 0) == column
    reply = [
        jnp.sum(jnp.where(mark, grid[m * columns : (m + 1) * columns], 0.0), axis=0, keepdims=True)
        for m in range(STEPS)
    ]
    record = record.astype(jnp.int32)
    offset = record % STEPS
    delayed = []
    for n in range(STEPS):
        value = jnp.where(offset == n, reply[0], 0.0)
        for m in range(1, n + 1):
            value = value + jnp.where(offset == n - m, reply[m], 0.0)
        delayed.append(value)
    delayed = jnp.concatenate(delayed + [jnp.zeros((8 - STEPS, sent), jnp.float32)], axis=0)
    key = owner * records + record // STEPS
    gather = (iota((owners * records, sent), 0) == key).astype(jnp.float32)
    part = lax.dot_general(
        delayed, gather, NT, preferred_element_type=jnp.float32, precision=lax.Precision.HIGHEST
    )
    for s in range(owners):
        share = part[:STEPS, s * records : (s + 1) * records]
        out_ref[s] = share if earlier is None else share + earlier[s]


def respond(owners, ranks, records, strain, columns, half, *earlier):
    vmem = pl.BlockSpec(memory_space=pltpu.VMEM)
    operands = (strain, columns, *half, *earlier)
    return pl.pallas_call(
        functools.partial(response_kernel, owners, ranks, records),
        out_shape=jax.ShapeDtypeStruct((owners, STEPS, records), jnp.float32),
        in_specs=[vmem] * len(operands),
        out_specs=vmem,
        compiler_params=pltpu.CompilerParams(vmem_limit_bytes=40 << 20),
        name="respond",
    )(*operands)


def partner(index, length, turn):
    if turn is None:
        return index
    other = index + 1 if index % 2 == turn else index - 1
    return other if 0 <= other < length else None


def exchange(value, gxs, gys, turn_x, turn_y):
    pairs = []
    for i in range(gxs):
        for j in range(gys):
            x, y = partner(i, gxs, turn_x), partner(j, gys, turn_y)
            if x is not None and y is not None:
                pairs.append((i * gys + j, x * gys + y))
    return lax.ppermute(value, OWNERS_AXES, pairs)


def body(displacement, previous, first_lame, shear_modulus, buoyancy, tile_column, rupture_tiles, slip_offsets, slip_panels):
    gxs, gys = lax.axis_size("gx"), lax.axis_size("gy")
    owners = gxs * gys
    nx, ny, nz = shear_modulus.shape
    halo = STEPS
    slots = tile_column.shape[0]
    records, listed = rupture_tiles.shape
    entries = records * listed
    ranks = entries // owners
    components = slip_panels.shape[2]

    waves = (displacement, previous, first_lame, shear_modulus, buoyancy)
    turns_y = range(1 if gys == 2 else 2)
    sent = prepare(halo, len(turns_y), *waves)
    ways = [(0, None), (1, None)] + [(x, q) for q in turns_y for x in (None, 0, 1)]
    slip_panels, sent = lax.optimization_barrier((slip_panels, sent))
    halos = [exchange(value, gxs, gys, *way) for value, way in zip(sent, ways)]

    panels = slip_panels.transpose(0, 2, 1, 3)
    payload = pack(owners, slots, ranks, rupture_tiles, slip_offsets, panels)
    arrived = lax.all_to_all(payload, OWNERS_AXES, split_axis=0, concat_axis=0, tiled=True)

    final, strain = stencil(halo, *waves, halos)
    arrived, strain = lax.optimization_barrier((arrived, strain))
    other = lax.ppermute(arrived, "comp", [(0, 1), (1, 0)])
    columns = tile_column.reshape(1, slots)
    partial = respond(owners, ranks, records, strain, columns, unpack(owners, ranks, components, arrived))
    partial = respond(owners, ranks, records, strain, columns, unpack(owners, ranks, components, other), partial)
    shares = lax.all_to_all(partial, OWNERS_AXES, split_axis=0, concat_axis=0, tiled=True)
    return final, jnp.sum(shares, axis=0).T[None]


def solution(mesh):
    in_specs = (
        P("comp", None, ("site", "gx"), "gy", None),
        P("comp", None, ("site", "gx"), "gy", None),
        P(("site", "gx"), "gy", None),
        P(("site", "gx"), "gy", None),
        P(("site", "gx"), "gy", None),
        P(("site", "gx", "gy")),
        P(("site", "gx", "gy"), None),
        P(("site", "gx", "gy"), None),
        P(("site", "gx", "gy"), None, None, None),
    )
    out_specs = (P("comp", None, ("site", "gx"), "gy", None), P("comp", ("site", "gx", "gy"), None))
    return jax.shard_map(body, mesh=mesh, in_specs=in_specs, out_specs=out_specs, check_vma=False)
```

```python
import functools

import jax
import jax.numpy as jnp
from jax import lax
from jax.experimental import pallas as pl
from jax.experimental.pallas import tpu as pltpu
from jax.sharding import PartitionSpec as P

STEPS = 4
TIME_STEP = 0.12
LANES = 128
PAD = 8
OWNERS_AXES = ("gx", "gy")
FIELDS = 9
NT = (((1,), (1,)), ((), ()))


def iota(shape, dim):
    return lax.broadcasted_iota(jnp.int32, shape, dim)


def owner_index():
    return lax.axis_index("gx") * lax.axis_size("gy") + lax.axis_index("gy")


def pack_kernel(owners, slots, ranks, tiles_ref, offsets_ref, panels_ref, arrive, out_ref, meta_ref=None):
    rows, cols = tiles_ref.shape
    entries = rows * cols
    core = lax.axis_index("comp")
    me = owner_index()
    tiles = tiles_ref[...]
    shift = slots.bit_length() - 1
    fields = jnp.concatenate([tiles >> shift, tiles & (slots - 1), offsets_ref[...]], axis=0)
    spread = (iota((cols, entries), 1) % cols == iota((cols, entries), 0)).astype(jnp.bfloat16)
    wide = jnp.dot(fields.astype(jnp.float32).astype(jnp.bfloat16), spread, preferred_element_type=jnp.float32)
    lane_row = iota((rows, entries), 1) // cols
    keep = lane_row == iota((rows, entries), 0)
    source, slot, offset = [
        jnp.sum(jnp.where(keep, wide[i * rows : (i + 1) * rows], 0.0), axis=0, keepdims=True) for i in range(3)
    ]
    record = (iota((1, entries), 1) // cols).astype(jnp.float32) * STEPS + offset
    chosen = source == iota((owners, entries), 0).astype(jnp.float32)
    before = (iota((entries, entries), 0) < iota((entries, entries), 1)).astype(jnp.bfloat16)
    counts = jnp.dot(chosen.astype(jnp.bfloat16), before, preferred_element_type=jnp.float32)
    rank = jnp.sum(jnp.where(chosen, counts, 0.0), axis=0, keepdims=True).astype(jnp.int32) - core * ranks
    mine = (rank >= 0) & (rank < ranks)
    place = jnp.where(mine, source.astype(jnp.int32) * ranks + rank, -1)
    sent = owners * ranks
    select = (iota((sent, entries), 0) == place).astype(jnp.bfloat16)
    blocks = out_ref.shape[0]
    length = sent // blocks
    components = panels_ref.shape[1]
    arrive()
    for i in range(components):
        part = jnp.dot(select, panels_ref[:, i].reshape(entries, LANES), preferred_element_type=jnp.float32).astype(jnp.bfloat16)
        out_ref[:, i * length : (i + 1) * length, :] = part.reshape(blocks, length, LANES)
    group = LANES // ranks
    lane = jnp.where(mine, rank + ranks * (me % group), -1)
    marks = (iota((LANES, entries), 0) == lane).astype(jnp.bfloat16)
    meta = []
    for value in (slot, record):
        table = jnp.where(chosen, value, 0.0).astype(jnp.bfloat16)
        meta.append(lax.dot_general(table, marks, NT, preferred_element_type=jnp.float32).astype(jnp.bfloat16))
    if meta_ref is None:
        tail = jnp.concatenate([m.reshape(owners, 1, LANES) for m in meta] * 4, axis=1)
        out_ref[:, components * length :, :] = tail
    else:
        for k in range(2):
            meta_ref[k] = meta[k]


META_ROWS = 8


def unpack(owners, ranks, components, arrived):
    if ranks % 16 == 0:
        return (arrived,)
    body = arrived[:, : components * ranks]
    meta = arrived[:, components * ranks :].transpose(1, 0, 2)
    body = body.reshape(owners, components, ranks, LANES).transpose(1, 0, 2, 3)
    return body.reshape(1, components * owners * ranks, LANES), meta


def planes_for(field, halo):
    return halo if field < 3 or field in (6, 7) else halo - 1


def coded_planes(halo):
    return sum(planes_for(f, halo) + (f < 6) for f in range(FIELDS))


def encode(halo, read, write):
    at = 0
    for field in range(FIELDS):
        near = None
        for k in range(planes_for(field, halo)):
            value = read(field, k)
            if field >= 6:
                parts = [value.astype(jnp.bfloat16)]
            elif near is None:
                high = value.astype(jnp.bfloat16)
                low = (value - high.astype(jnp.float32)).astype(jnp.bfloat16)
                near = high.astype(jnp.float32) + low.astype(jnp.float32)
                parts = [high, low]
            else:
                step = (value - near).astype(jnp.bfloat16)
                near = near + step.astype(jnp.float32)
                parts = [step]
            for part in parts:
                write(at, part)
                at += 1


def decode(halo, read, write):
    at = 0
    for field in range(FIELDS):
        near = None
        for k in range(planes_for(field, halo)):
            value = read(at).astype(jnp.float32)
            at += 1
            if field < 6:
                if near is None:
                    value = value + read(at).astype(jnp.float32)
                    at += 1
                else:
                    value = near + value
                near = value
            write(field, k, value)


def prepare_kernel(halo, fields, *outs):
    _, nx, ny, nz = fields.shape
    odd_x, odd_y = lax.axis_index("gx") % 2, lax.axis_index("gy") % 2

    def coded(p, rows, target):
        def write(at, value):
            target[at] = value

        encode(halo, lambda f, k: fields[f, jnp.where(odd_x == p, nx - 1 - k, k), rows, :], write)

    for p in range(2):
        coded(p, pl.ds(0, ny), outs[p])

    def edge(rows, targets):
        targets[0][...] = fields[:, :, rows, :]
        for p in range(2):
            coded(p, rows, targets[1 + p])

    for q, targets in enumerate((outs[2:5], outs[5:8])):
        if targets:
            pl.when(odd_y == q)(functools.partial(edge, pl.ds(ny - halo, halo), targets))
            pl.when(odd_y != q)(functools.partial(edge, pl.ds(0, halo), targets))


def opening_kernel(halo, owners, slots, ranks, sides, *refs):
    disp, prev, lam, mu, buoy, tiles, offsets, panels = refs[:8]
    fields, own_tiles, own_offsets, own_panels, sem = refs[-5:]
    outs = refs[8:-5]
    pairs = (
        (tiles, own_tiles),
        (offsets, own_offsets),
        (panels, own_panels),
        (disp.at[0], fields.at[pl.ds(0, 3)]),
        (prev.at[0], fields.at[pl.ds(3, 3)]),
        (lam, fields.at[6]),
        (mu, fields.at[7]),
        (buoy, fields.at[8]),
    )
    copies = [pltpu.make_async_copy(source, target, sem.at[i]) for i, (source, target) in enumerate(pairs)]
    for copy in copies:
        copy.start()
    copies[0].wait()
    copies[1].wait()
    pack_kernel(owners, slots, ranks, own_tiles, own_offsets, own_panels, copies[2].wait, *outs[sides:])
    for copy in copies[3:]:
        copy.wait()
    prepare_kernel(halo, fields, *outs[:sides])


def opening(halo, ways, owners, slots, ranks, waves, tiles, offsets, panels):
    nx, ny, nz = waves[2].shape
    vmem, anywhere = pl.BlockSpec(memory_space=pltpu.VMEM), pl.BlockSpec(memory_space=pltpu.HBM)
    count, components, sent = coded_planes(halo), panels.shape[1], owners * ranks
    edge = [jax.ShapeDtypeStruct((FIELDS, nx, halo, nz), jnp.float32)]
    edge += [jax.ShapeDtypeStruct((count, halo, nz), jnp.bfloat16)] * 2
    shapes = [jax.ShapeDtypeStruct((count, ny, nz), jnp.bfloat16)] * 2 + edge * ways
    sides = len(shapes)
    if ranks % 16 == 0:
        shapes.append(jax.ShapeDtypeStruct((owners, components * ranks + META_ROWS, LANES), jnp.bfloat16))
    else:
        shapes.append(jax.ShapeDtypeStruct((1, components * sent, LANES), jnp.bfloat16))
        shapes.append(jax.ShapeDtypeStruct((2, owners, LANES), jnp.bfloat16))
    outs = pl.pallas_call(
        functools.partial(opening_kernel, halo, owners, slots, ranks, sides),
        out_shape=shapes,
        in_specs=[anywhere] * 8,
        out_specs=[vmem] * len(shapes),
        scratch_shapes=[
            pltpu.VMEM((FIELDS, nx, ny, nz), jnp.float32),
            pltpu.VMEM(tiles.shape, jnp.int32),
            pltpu.VMEM(offsets.shape, jnp.int32),
            pltpu.VMEM(panels.shape, jnp.bfloat16),
            pltpu.SemaphoreType.DMA((8,)),
        ],
        name="opening",
    )(*waves, tiles, offsets, panels)
    if ranks % 16 == 0:
        return outs[:sides], outs[sides]
    body, meta = outs[sides:]
    body = body.reshape(components, owners, ranks, LANES).transpose(1, 0, 2, 3)
    body = body.reshape(owners, components * ranks, LANES)
    return outs[:sides], jnp.concatenate([body, meta.transpose(1, 0, 2)], axis=1)


def shifted_up(value, dim):
    return pltpu.roll(value, value.shape[dim] - 1, dim)


def stencil_kernel(halo, *refs):
    disp, prev, lam, mu, buoy = refs[:5]
    halos, (out_ref, strain_ref) = refs[5:-7], refs[-7:-5]
    wave, first, second, scale = refs[-5:-1]
    nx, ny, nz = lam.shape
    tall = ny + 2 * PAD
    odd_x, odd_y = lax.axis_index("gx") % 2, lax.axis_index("gy") % 2
    own_x, own_y = pl.ds(halo, nx), pl.ds(PAD, ny)
    targets = [wave.at[0, i] for i in range(3)] + [wave.at[1, i] for i in range(3)] + [first, second, scale]

    def put(field, xs, ys, value):
        targets[field][xs, ys, :] = value * (TIME_STEP * TIME_STEP) if field == 8 else value

    def spread(p, ys, read):
        def write(field, k, value):
            put(field, jnp.where(odd_x == p, halo + nx + k, halo - 1 - k), ys, value)

        decode(halo, read, write)

    owns = [disp[0, i] for i in range(3)] + [prev[0, i] for i in range(3)] + [lam[...], mu[...], buoy[...]]
    for f, own in enumerate(owns):
        put(f, own_x, own_y, own)
    for p in range(2):
        spread(p, own_y, lambda at, p=p: halos[p][at])
    for upper, ys in ((True, pl.ds(PAD + ny, halo)), (False, pl.ds(PAD - halo, halo))):

        def side(i, at, upper=upper):
            taken = (odd_y == 0) if upper else (odd_y != 0)
            value = halos[2 + i][at].astype(jnp.float32)
            return jnp.where(taken, value, halos[5 + i][at].astype(jnp.float32) if len(halos) > 5 else 0.0)

        for f in range(FIELDS):
            put(f, own_x, ys, side(0, f))
        for p in range(2):
            spread(p, ys, lambda at, p=p, side=side: side(1 + p, at))

    lane = iota((tall, nz), 1)
    not_last, not_first = lane < nz - 1, lane > 0

    def fields(cur, x):
        base = [wave[cur, i, x] for i in range(3)]
        nxt = [wave[cur, i, x + 1] for i in range(3)]
        dx = [n - b for n, b in zip(nxt, base)]
        dy = [shifted_up(b, 0) - b for b in base]
        dz = [jnp.where(not_last, shifted_up(b, 1), 0.0) - b for b in base]
        normal = [dx[0], dy[1], dz[2]]
        twice = [dy[0] + dx[1], dz[0] + dx[2], dz[1] + dy[2]]
        m = second[x]
        volume = first[x] * (normal[0] + normal[1] + normal[2])
        m2 = m + m
        stress = [volume + m2 * e for e in normal] + [m * e for e in twice]
        return base, normal, twice, stress

    def back_y(v):
        return v - pltpu.roll(v, 1, 0)

    def back_z(v):
        return v - jnp.where(not_first, pltpu.roll(v, 1, 1), 0.0)

    def plane(step, cur, own, x, carry):
        base, normal, twice, stress = fields(cur, x)
        if own:
            rows = pl.ds(pl.multiple_of(step * nx * ny + (x - halo) * ny, ny), ny)
            for e, value in enumerate(normal + [0.5 * t for t in twice]):
                strain_ref[rows, e * nz : (e + 1) * nz] = value[PAD : PAD + ny].astype(jnp.bfloat16)
        xx, yy, zz, xy, xz, yz = stress
        forces = [
            (xx - carry[0]) + back_y(xy) + back_z(xz),
            (xy - carry[1]) + back_y(yy) + back_z(yz),
            (xz - carry[2]) + back_y(yz) + back_z(zz),
        ]
        for i in range(3):
            value = 2.0 * base[i] - wave[1 - cur, i, x] + scale[x] * forces[i]
            if step == STEPS - 1:
                out_ref[0, i, x - halo] = value[PAD : PAD + ny]
            else:
                wave[1 - cur, i, x] = value
        return xx, xy, xz

    for step in range(STEPS):
        cur = step % 2
        reach = STEPS - 1 - step
        begin, end = halo - reach, halo + nx + reach
        stress = fields(cur, begin - 1)[3]
        carry = (stress[0], stress[3], stress[4])
        for lo, hi, own in ((begin, halo, False), (halo, halo + nx, True), (halo + nx, end, False)):
            if hi > lo:
                carry = lax.fori_loop(lo, hi, functools.partial(plane, step, cur, own), carry)


def stencil(halo, disp, prev, lam, mu, buoy, halos):
    nx, ny, nz = lam.shape
    tall, wide = ny + 2 * PAD, nx + 2 * halo
    vmem = pl.BlockSpec(memory_space=pltpu.VMEM)
    operands = (disp, prev, lam, mu, buoy, *halos)
    return pl.pallas_call(
        functools.partial(stencil_kernel, halo),
        out_shape=(
            jax.ShapeDtypeStruct((1, 3, nx, ny, nz), jnp.float32),
            jax.ShapeDtypeStruct((STEPS * nx * ny, 6 * nz), jnp.bfloat16),
        ),
        in_specs=[vmem] * len(operands),
        out_specs=(vmem, vmem),
        scratch_shapes=[pltpu.VMEM((2, 3, wide, tall, nz), jnp.float32)]
        + [pltpu.VMEM((wide, tall, nz), jnp.float32)] * 3
        + [pltpu.SMEM((1,), jnp.int32)],
        compiler_params=pltpu.CompilerParams(vmem_limit_bytes=40 << 20),
        cost_estimate=pl.CostEstimate(flops=10**10, transcendentals=10**8, bytes_accessed=10**8),
        name="stencil",
    )(*operands)


def response_kernel(owners, ranks, records, strain_ref, column_ref, *refs):
    points = column_ref.shape[1]
    sent = owners * ranks
    group = LANES // ranks
    columns = strain_ref.shape[0] // STEPS
    pan, out_ref = refs[0], refs[-1]
    friendly = ranks % 16 == 0
    earlier = refs[-2] if len(refs) > (2 if friendly else 3) else None
    length = sent // pan.shape[0]
    rows = []
    for k in range(2):
        table = pan[:, 6 * length + k, :] if friendly else refs[1][k]
        table = table.astype(jnp.float32)
        parts = [
            jnp.sum(table[g * group : (g + 1) * group], axis=0, keepdims=True) for g in range(owners // group)
        ]
        rows.append(jnp.concatenate(parts, axis=1))
    slot, record = rows
    owner = iota((1, sent), 1) // ranks
    spread = (iota((points, sent), 0) == slot.astype(jnp.int32)).astype(jnp.bfloat16)
    table = jnp.broadcast_to(column_ref[...].astype(jnp.float32), (8, points)).astype(jnp.bfloat16)
    column = jnp.dot(table, spread, preferred_element_type=jnp.float32)[:1].astype(jnp.int32)
    grid = None
    for i in range(3):
        right = jnp.concatenate(
            [pan[:, (2 * i + k) * length : (2 * i + k + 1) * length, :].reshape(sent, LANES) for k in range(2)],
            axis=1,
        )
        left = strain_ref[:, 2 * i * LANES : (2 * i + 2) * LANES]
        term = lax.dot_general(left, right, NT, preferred_element_type=jnp.float32)
        grid = term if grid is None else grid + term
    mark = iota((columns, sent), 0) == column
    reply = [
        jnp.sum(jnp.where(mark, grid[m * columns : (m + 1) * columns], 0.0), axis=0, keepdims=True)
        for m in range(STEPS)
    ]
    record = record.astype(jnp.int32)
    offset = record % STEPS
    delayed = []
    for n in range(STEPS):
        value = jnp.where(offset == n, reply[0], 0.0)
        for m in range(1, n + 1):
            value = value + jnp.where(offset == n - m, reply[m], 0.0)
        delayed.append(value)
    delayed = jnp.concatenate(delayed + [jnp.zeros((8 - STEPS, sent), jnp.float32)], axis=0)
    key = owner * records + record // STEPS
    gather = (iota((owners * records, sent), 0) == key).astype(jnp.float32)
    part = lax.dot_general(
        delayed, gather, NT, preferred_element_type=jnp.float32, precision=lax.Precision.HIGHEST
    )
    for s in range(owners):
        share = part[:STEPS, s * records : (s + 1) * records]
        out_ref[s] = share if earlier is None else share + earlier[s]


def respond(owners, ranks, records, strain, columns, half, *earlier):
    vmem = pl.BlockSpec(memory_space=pltpu.VMEM)
    operands = (strain, columns, *half, *earlier)
    return pl.pallas_call(
        functools.partial(response_kernel, owners, ranks, records),
        out_shape=jax.ShapeDtypeStruct((owners, STEPS, records), jnp.float32),
        in_specs=[vmem] * len(operands),
        out_specs=vmem,
        compiler_params=pltpu.CompilerParams(vmem_limit_bytes=40 << 20),
        name="respond",
    )(*operands)


def partner(index, length, turn):
    if turn is None:
        return index
    other = index + 1 if index % 2 == turn else index - 1
    return other if 0 <= other < length else None


def exchange(value, gxs, gys, turn_x, turn_y):
    pairs = []
    for i in range(gxs):
        for j in range(gys):
            x, y = partner(i, gxs, turn_x), partner(j, gys, turn_y)
            if x is not None and y is not None:
                pairs.append((i * gys + j, x * gys + y))
    return lax.ppermute(value, OWNERS_AXES, pairs)


def body(displacement, previous, first_lame, shear_modulus, buoyancy, tile_column, rupture_tiles, slip_offsets, slip_panels):
    gxs, gys = lax.axis_size("gx"), lax.axis_size("gy")
    owners = gxs * gys
    nx, ny, nz = shear_modulus.shape
    halo = STEPS
    slots = tile_column.shape[0]
    records, listed = rupture_tiles.shape
    entries = records * listed
    ranks = entries // owners
    components = slip_panels.shape[2]

    waves = (displacement, previous, first_lame, shear_modulus, buoyancy)
    turns_y = range(1 if gys == 2 else 2)
    panels = slip_panels.transpose(0, 2, 1, 3)
    sent, payload = opening(
        halo, len(turns_y), owners, slots, ranks, waves, rupture_tiles, slip_offsets, panels
    )
    ways = [(0, None), (1, None)] + [(x, q) for q in turns_y for x in (None, 0, 1)]
    halos = [exchange(value, gxs, gys, *way) for value, way in zip(sent, ways)]

    arrived = lax.all_to_all(payload, OWNERS_AXES, split_axis=0, concat_axis=0, tiled=True)

    final, strain = stencil(halo, *waves, halos)
    arrived, strain = lax.optimization_barrier((arrived, strain))
    other = lax.ppermute(arrived, "comp", [(0, 1), (1, 0)])
    columns = tile_column.reshape(1, slots)
    partial = respond(owners, ranks, records, strain, columns, unpack(owners, ranks, components, arrived))
    partial = respond(owners, ranks, records, strain, columns, unpack(owners, ranks, components, other), partial)
    shares = lax.all_to_all(partial, OWNERS_AXES, split_axis=0, concat_axis=0, tiled=True)
    return final, jnp.sum(shares, axis=0).T[None]


def solution(mesh):
    in_specs = (
        P("comp", None, ("site", "gx"), "gy", None),
        P("comp", None, ("site", "gx"), "gy", None),
        P(("site", "gx"), "gy", None),
        P(("site", "gx"), "gy", None),
        P(("site", "gx"), "gy", None),
        P(("site", "gx", "gy")),
        P(("site", "gx", "gy"), None),
        P(("site", "gx", "gy"), None),
        P(("site", "gx", "gy"), None, None, None),
    )
    out_specs = (P("comp", None, ("site", "gx"), "gy", None), P("comp", ("site", "gx", "gy"), None))
    return jax.shard_map(body, mesh=mesh, in_specs=in_specs, out_specs=out_specs, check_vma=False)
```
